512 devices in a mesh: shard: 64 (over z, y), replica: 8 (over x, core).
Axes of the slice: x: 4, y: 8, z: 8, core: 2. Of those that a mesh axis runs over, the one named last changes fastest.
Arguments:
- request_rows: int32 [8, 64, 128], P('replica', 'shard'), may hold values from 0 to 1023, as said below
- token_slot: int32 [8, 8192], P('replica', 'shard'), may hold values from 0 to 127, as said below
- seq_lengths: int32 [8, 64, 8], P('replica', 'shard'), may hold values from 1 to 48, 128 in all within a row
- cotangent: bfloat16 [8, 8192, 256], P('replica', 'shard'), may hold values from -6 to 6
- table_slab: float32 [65536, 256], P('shard'), may hold values from -6 to 6
- adagrad_state: float32 [65536], P('shard'), may hold values from 0.1 to 1
- w_uvqk: bfloat16 [256, 1024], replicated, may hold values from -0.375 to 0.375
- w_out: bfloat16 [256, 256], replicated, may hold values from -0.375 to 0.375
- norm_gain: float32 [256], replicated, may hold values from 0.1 to 1.9
- out_gain: float32 [256], replicated, may hold values from 0.1 to 1.9
Outputs:
- row_update: float32 [65536, 256], P('shard')
- state_new: float32 [65536], P('shard')
- grad_uvqk: float32 [256, 1024], replicated
- grad_out: float32 [256, 256], replicated
- grad_gains: float32 [2, 256], replicated
The draws below stay inside these ranges and needn't reach their ends.
Inputs may be any that keep to these rules, and one draw needn't show every extreme that they name: `request_rows`: on each device the rows asked of one owner (slots j with one value of j // 2) are distinct. `token_slot`: each token names one slot of its own device. For each owner the named slots are the first ones of its 2 slots, every such slot is named by some token, and on every device some owner has all 2 slots named. Slots that no token names still ask for a row (each a distinct one); their gradient is zero. `seq_lengths`: the lengths of one device sum to 128; the longest is exactly 48.
All inputs are finite; a program needn't handle non-finite values.
Results may differ from the reference program's by a relative error of at most 0.014.
Values may be sent and summed in bfloat16 or wider, within the bound.
A program may use at most 64 MiB of HBM per device.

```python
import math
import jax
import jax.numpy as jnp
import numpy as np
from jax import lax

E = 256
HEADS = 4
TOK_DEV = 128
SEQS = 8
MAXLEN = 48
ROWS_DEV = 1024
TOKENS = 8192
ROWS_TOTAL = 65536
N_SHARD = 64
N_REPLICA = 8


def device_plan(device_key):
    capacity = TOK_DEV // N_SHARD
    split_keys = jax.random.split(device_key, 6)
    counts = jax.random.randint(split_keys[0], (N_SHARD,), 1, capacity + 1)
    full_owner = jax.random.randint(split_keys[1], (), 0, N_SHARD)
    counts = jnp.where(jnp.arange(N_SHARD) == full_owner, capacity, counts)
    slot_index = jnp.arange(TOK_DEV, dtype=jnp.int32)
    owner_of = slot_index // capacity
    in_bucket = slot_index % capacity
    is_live = in_bucket < counts[owner_of]
    row_start = jax.random.randint(split_keys[2], (N_SHARD,), 0, ROWS_DEV)
    row_step = 2 * jax.random.randint(split_keys[3], (N_SHARD,), 0, ROWS_DEV // 2) + 1
    asked = ((row_start[owner_of] + row_step[owner_of] * in_bucket) % ROWS_DEV).astype(jnp.int32)
    live_first = jnp.argsort(1 - is_live.astype(jnp.int32), stable=True).astype(jnp.int32)
    live_count = jnp.sum(is_live.astype(jnp.int32))
    chosen = jax.random.randint(split_keys[4], (TOK_DEV,), 0, live_count)
    source_slot = jnp.where(slot_index < live_count, slot_index, chosen)
    token_slots = live_first[source_slot]
    shuffle = jax.random.permutation(split_keys[5], TOK_DEV)
    return (asked, token_slots[shuffle].astype(jnp.int32))


def slot_plan(key):
    device_keys = jax.random.split(jax.random.fold_in(key, 11), N_REPLICA * N_SHARD)
    asked, token_slots = jax.vmap(device_plan)(device_keys)
    return (asked, token_slots)


def draw_request_rows(key, part):
    asked, token_slots = slot_plan(key)
    return asked.reshape(N_REPLICA, N_SHARD, TOK_DEV)


def draw_token_slot(key, part):
    asked, token_slots = slot_plan(key)
    return token_slots.reshape(N_REPLICA, N_SHARD * TOK_DEV)


def levels(key, dims, cuts, smallest, largest):
    def one(position, parts):
        heights = jax.random.uniform(jax.random.fold_in(jax.random.fold_in(key, 6), position), (parts,), jnp.float32, smallest / len(cuts), largest / len(cuts))
        return jnp.repeat(jnp.exp(heights), dims[position] // parts).reshape((-1,) + (1,) * (len(dims) - position - 1))

    gain = one(*cuts[0])
    for cut in cuts[1:]:
        gain = gain * one(*cut)
    return gain


def profile(count, total, most, slope):
    portions = [(1 << 20) // math.isqrt(standing ** slope) + 1 for standing in range(2, count + 1)]
    rest, given = total - most - (count - 1), [1] * (count - 1)
    while rest > 0:
        movable = [i for i in range(count - 1) if given[i] < most]
        whole, left = sum([portions[i] for i in movable]), rest
        for i in movable:
            extra = min(most - given[i], max(1, left * portions[i] // whole), rest)
            given[i] = given[i] + extra
            rest = rest - extra
    return np.array([most] + given)


def ragged(stream_key, count, total, bound, skew):
    if count == 2:
        one = jax.random.randint(stream_key, (), max(1, total - bound), min(bound, total - 1) + 1)
        return jnp.stack([one, total - one])
    tallies = jnp.asarray(profile(count, total, bound, skew), jnp.int32)
    couples = (count - 1) // 2
    donor, sink = tallies[1:1 + 2 * couples:2], tallies[2:2 + 2 * couples:2]
    room = jnp.minimum(donor - 1, bound - sink)
    shifted = jax.random.randint(jax.random.fold_in(stream_key, 1), (couples,), 0, 1 << 20) % (room + 1)
    tallies = tallies.at[1:1 + 2 * couples:2].set(donor - shifted).at[2:2 + 2 * couples:2].set(sink + shifted)
    return tallies[jax.random.permutation(jax.random.fold_in(stream_key, 2), count)]


def gaussian(stream_key, extent, deviation, reach, cuts=(), held_as=jnp.bfloat16):
    gain = levels(stream_key, extent, cuts, -0.22, 0.18) if cuts else 1.0
    values = jax.random.normal(stream_key, extent, jnp.float32) * deviation * gain
    return jnp.minimum(jnp.maximum(values, -reach), reach).astype(held_as)


def setup_inputs(seed: int = 0) -> dict:
    key_list = jax.random.split(jax.random.key(seed), 11)
    request_rows = draw_request_rows(jax.random.fold_in(key_list[10], 71), 0)
    token_slot = draw_token_slot(jax.random.fold_in(key_list[10], 71), 0)
    seq_lengths = jax.vmap(lambda own: ragged(own, SEQS, TOK_DEV, MAXLEN, 2))(jax.random.split(key_list[2], N_REPLICA * N_SHARD)).reshape((N_REPLICA, N_SHARD, SEQS)).astype(jnp.int32)
    cotangent = gaussian(key_list[3], (N_REPLICA, TOKENS, E), 1.0, 6.0, ((0, 8), (1, 64)))
    table_slab = gaussian(key_list[4], (ROWS_TOTAL, E), 1.0, 6.0, ((0, 64),), jnp.float32)
    adagrad_state = jnp.clip(jnp.exp(math.log(1.0) - 2.3025851 * jax.random.uniform(key_list[5], (ROWS_TOTAL,), jnp.float32) ** levels(key_list[5], (ROWS_TOTAL,), ((0, 64),), -0.2, 0.2)), 0.1, 1.0)
    w_uvqk = gaussian(key_list[6], (E, 4 * E), E ** -0.5, 0.375)
    w_out = gaussian(key_list[7], (E, E), E ** -0.5, 0.375)
    norm_gain = jnp.clip(1.0 + 0.18 * jax.random.normal(key_list[8], (E,), jnp.float32), 0.1, 1.9)
    out_gain = jnp.clip(1.0 + 0.18 * jax.random.normal(key_list[9], (E,), jnp.float32), 0.1, 1.9)
    return {"request_rows": request_rows, "token_slot": token_slot, "seq_lengths": seq_lengths, "cotangent": cotangent, "table_slab": table_slab, "adagrad_state": adagrad_state, "w_uvqk": w_uvqk, "w_out": w_out, "norm_gain": norm_gain, "out_gain": out_gain}


epsilon = 1e-08
learn_rate = 0.5

def normalize(values):
    center = values - lax.optimization_barrier(jnp.mean(values, axis=1, keepdims=True))
    variance = lax.optimization_barrier(jnp.mean(center * center, axis=1, keepdims=True))
    return center * lax.rsqrt(variance + 1e-05)

def same_sequence(lengths, count):
    seq_ends = jnp.cumsum(lengths)
    positions = jnp.arange(count, dtype=jnp.int32)
    segment = lax.optimization_barrier(jnp.sum(positions[:, None] >= seq_ends[None, :], axis=1))
    return (segment[:, None] == segment[None, :]) & (positions[:, None] >= positions[None, :])

def hstu_layer(embedded, w_uvqk, w_out, norm_gain, out_gain, same_seq):
    count = embedded.shape[0]
    model_width = embedded.shape[1]
    head_width = model_width // HEADS
    normed = (normalize(embedded) * norm_gain).astype(jnp.bfloat16)
    projected = jax.nn.silu(jnp.dot(normed, w_uvqk, preferred_element_type=jnp.float32))
    gate_u = projected[:, :model_width]
    packed = projected[:, model_width:].astype(jnp.bfloat16).reshape(count, 3, HEADS, head_width)
    values = packed[:, 0].astype(jnp.float32)
    queries = packed[:, 1].astype(jnp.float32)
    key_rows = packed[:, 2].astype(jnp.float32)
    scores = jnp.einsum('qhd,khd->hqk', queries, key_rows) * head_width ** (-0.5)
    weights = jnp.where(same_seq[None], jax.nn.silu(scores) / MAXLEN, 0.0).astype(jnp.bfloat16)
    attended = jnp.einsum('hqk,khd->qhd', weights.astype(jnp.float32), values).reshape(count, model_width)
    gated = (normalize(attended) * out_gain * gate_u).astype(jnp.bfloat16)
    return embedded + jnp.dot(gated, w_out, preferred_element_type=jnp.float32)

def reference(request_rows, token_slot, seq_lengths, cotangent, table_slab, adagrad_state, w_uvqk, w_out, norm_gain, out_gain):
    capacity = TOK_DEV // N_SHARD
    owners = jnp.arange(TOK_DEV, dtype=jnp.int32) // capacity * ROWS_DEV
    slot_all = token_slot.reshape(N_REPLICA, N_SHARD, TOK_DEV)
    cotan_all = cotangent.reshape(N_REPLICA, N_SHARD, TOK_DEV, E)
    grad_scale = 1.0 / math.sqrt(TOK_DEV * N_SHARD * N_REPLICA)

    def device_step(state_carry, device_item):
        row_grads, dense_sums = state_carry
        asked_rows, slot_ids, lengths, cotan_rows = device_item
        flat_rows = owners + asked_rows.astype(jnp.int32)
        found_rows = table_slab[flat_rows].astype(jnp.bfloat16)
        embedded = found_rows[slot_ids].astype(jnp.float32)
        same_seq = same_sequence(lengths, TOK_DEV)

        def local_layer(first, second, third, fourth, fifth):
            return hstu_layer(first, second, third, fourth, fifth, same_seq)
        unused, pullback = jax.vjp(local_layer, embedded, w_uvqk, w_out, norm_gain, out_gain)
        token_grad, grad_one, grad_two, grad_norm, grad_gate = pullback(cotan_rows.astype(jnp.float32))
        slot_grad = jax.ops.segment_sum(token_grad, slot_ids, num_segments=TOK_DEV)
        row_grads = row_grads.at[flat_rows].add(slot_grad)
        dense_sums = (dense_sums[0] + grad_one.astype(jnp.float32) * grad_scale, dense_sums[1] + grad_two.astype(jnp.float32) * grad_scale, dense_sums[2] + jnp.stack([grad_norm, grad_gate]).astype(jnp.float32) * grad_scale)
        return ((row_grads, dense_sums), None)

    def replica_step(state_carry, replica_item):
        delta_sum, square_sum, dense_sums = state_carry
        initial = (jnp.zeros((ROWS_TOTAL, E), jnp.float32), dense_sums)
        (row_grads, dense_sums), unused = lax.scan(device_step, initial, replica_item)
        mean_square = lax.optimization_barrier(jnp.mean(row_grads * row_grads, axis=1))
        row_delta = -learn_rate * row_grads / jnp.sqrt(adagrad_state + mean_square + epsilon)[:, None]
        return ((delta_sum + row_delta, square_sum + mean_square, dense_sums), None)
    initial = (jnp.zeros((ROWS_TOTAL, E), jnp.float32), jnp.zeros((ROWS_TOTAL,), jnp.float32), (jnp.zeros((E, 4 * E), jnp.float32), jnp.zeros((E, E), jnp.float32), jnp.zeros((2, E), jnp.float32)))
    (delta_sum, square_sum, dense_sums), unused = lax.scan(replica_step, initial, (request_rows, slot_all, seq_lengths, cotan_all))
    return (delta_sum / N_REPLICA, adagrad_state + square_sum / N_REPLICA, dense_sums[0], dense_sums[1], dense_sums[2])
```

```python
import functools
import math

import jax
import jax.numpy as jnp
from jax import lax
from jax.experimental import pallas as pl
from jax.experimental.pallas import tpu as pltpu
from jax.sharding import PartitionSpec as P

HEADS = 4
MAXLEN = 48
SEQS = 8
EPSILON = 1e-08
LEARN_RATE = 0.5
E = 256
T = 128
F32 = jnp.float32
BF16 = jnp.bfloat16
MESH = pl.DeviceIdType.MESH


def far_first(n):
    return sorted(range(1, n), key=lambda d: -min(d, n - d))


def nn(a, b):
    return lax.dot_general(a, b, (((1,), (0,)), ((), ())), preferred_element_type=F32)


def nt(a, b):
    return lax.dot_general(a, b, (((1,), (1,)), ((), ())), preferred_element_type=F32)


def tn(a, b):
    return lax.dot_general(a, b, (((0,), (0,)), ((), ())), preferred_element_type=F32)


def iota(shape, dim):
    return lax.broadcasted_iota(jnp.int32, shape, dim)


def lane_mean(x):
    return jnp.sum(x, axis=1, keepdims=True) * (1.0 / x.shape[1])


def split2(x):
    high = x.astype(BF16)
    return high, (x - high.astype(F32)).astype(BF16)


def layer(x, cot, w_ref, wout_ref, ng, og, same):
    center = x - lane_mean(x)
    rstd = lax.rsqrt(lane_mean(center * center) + 1e-05)
    xhat = center * rstd
    normed = (xhat * ng).astype(BF16)
    pre = nn(normed, w_ref[...])
    sig = lax.logistic(pre)
    proj = pre * sig
    dsilu = sig * (1.0 + pre * (1.0 - sig))
    u = proj[:, :E]
    low = iota((T, 128), 1) < 64
    zero = jnp.zeros((T, 128), BF16)
    pairs, att = [], []
    for p in range(2):
        at = p * 128
        vp = proj[:, E + at : E + at + 128].astype(BF16)
        qp = proj[:, 2 * E + at : 2 * E + at + 128].astype(BF16)
        kp = proj[:, 3 * E + at : 3 * E + at + 128].astype(BF16)
        heads, total = [], None
        for h in range(2):
            mine = low if h == 0 else jnp.logical_not(low)
            qh, kh = jnp.where(mine, qp, zero), jnp.where(mine, kp, zero)
            s = nt(qh, kp) * 0.125
            sg = lax.logistic(s)
            weights = jnp.where(same, s * sg * (1.0 / MAXLEN), 0.0).astype(BF16)
            slope = jnp.where(same, sg * (1.0 + s * (1.0 - sg)) * (0.125 / MAXLEN), 0.0)
            part = nn(weights, jnp.where(mine, vp, zero))
            total = part if total is None else total + part
            heads.append((mine, qh, kh, weights, slope))
        pairs.append((vp, heads))
        att.append(total)
    attended = jnp.concatenate(att, axis=1)
    center2 = attended - lane_mean(attended)
    rstd2 = lax.rsqrt(lane_mean(center2 * center2) + 1e-05)
    ahat = center2 * rstd2
    gated = (ahat * og * u).astype(BF16)
    dgated = nt(cot, wout_ref[...]).astype(BF16).astype(F32)
    au = ahat * u
    dog = jnp.sum(dgated * au, axis=0, keepdims=True)
    dgo = dgated * og
    du = dgo * ahat
    dahat = dgo * u
    datt = rstd2 * (dahat - lane_mean(dahat) - ahat * lane_mean(dahat * ahat))
    datt = datt.astype(BF16)
    dvs, dqs, dks = [], [], []
    for p in range(2):
        vp, heads = pairs[p]
        dp = datt[:, p * 128 : p * 128 + 128]
        dv = dq = dk = None
        for mine, qh, kh, weights, slope in heads:
            dh = jnp.where(mine, dp, zero)
            dw = nt(dh, vp).astype(BF16).astype(F32)
            ds = (dw * slope).astype(BF16)
            a, b, c = tn(weights, dh), nn(ds, kh), tn(ds, qh)
            dv, dq, dk = (a, b, c) if dv is None else (dv + a, dq + b, dk + c)
        dvs.append(dv)
        dqs.append(dq)
        dks.append(dk)
    rounded = [t.astype(BF16).astype(F32) for t in (*dvs, *dqs, *dks)]
    dproj = jnp.concatenate([du, *rounded], axis=1)
    dpre = (dproj * dsilu).astype(BF16)
    dnormed = nt(dpre, w_ref[...]).astype(BF16).astype(F32)
    dng = jnp.sum(dnormed * xhat, axis=0, keepdims=True)
    dxhat = dnormed * ng
    dx = rstd * (dxhat - lane_mean(dxhat) - xhat * lane_mean(dxhat * xhat)) + cot.astype(F32)
    return dx, normed, dpre, gated, dng, dog


def step_kernel(
    nz, ny, nx,
    lens, ids_in, slots_in, cot_in, table_in, state_in, w_in, wout_in, ng_in, og_in,
    rows_out, state_out, fin_out, gains_out,
    iz_s, iz, iy, a_s, b_r, c_s, d_r, e_s, e_r, f_s, g_r, oht, wanted,
    dall, mall, wacc, w1_s, w1_r, acc2, w2_s, w2_r, w3_s, w3_r, w4, fin,
    ga_c, ga_x, ga_z, ga_y,
    zs, zr, ys, yr, xs, xr, cs, cr,
):
    cap = T // (nz * ny)
    zb, yb = T // nz, T // ny
    lcap, lny, lnz = int(math.log2(cap)), int(math.log2(ny)), int(math.log2(nz))
    lzb, lyb = int(math.log2(zb)), int(math.log2(yb))
    shard, rep = lax.axis_index("shard"), lax.axis_index("replica")
    z, y = shard // ny, lax.rem(shard, ny)
    x, c = rep // 2, lax.rem(rep, 2)
    other = 1 - c
    zpeer = lambda d: {"shard": lax.rem(z + d, nz) * ny + y}
    ypeer = lambda d: {"shard": z * ny + lax.rem(y + d, ny)}
    xpeer = lambda d: {"replica": lax.rem(x + d, nx) * 2 + c}
    cpeer = {"replica": x * 2 + other}
    zd, yd, xd = far_first(nz), far_first(ny), far_first(nx)

    def remote(src, dst, ssem, rsem, peer):
        return pltpu.make_async_remote_copy(
            src_ref=src, dst_ref=dst, send_sem=ssem, recv_sem=rsem,
            device_id=peer, device_id_type=MESH,
        )

    pending = []

    def start(copies):
        for copy in copies:
            copy.start()
        pending.extend(copies)
        return copies

    def arrive(copies):
        for copy in copies:
            copy.wait_recv()

    def along_z(k, src, dst):
        return start([remote(src(lax.rem(z + d, nz), d), dst(d), zs.at[k, d], zr.at[k, d], zpeer(d)) for d in zd])

    def along_y(k, src, dst):
        return start([remote(src(lax.rem(y + d, ny), d), dst(d), ys.at[k, d], yr.at[k, d], ypeer(d)) for d in yd])

    def along_x(k, src, dst):
        return start([remote(src(lax.rem(x + d, nx), d), dst(d), xs.at[k, d], xr.at[k, d], xpeer(d)) for d in xd])

    def across(k, src, dst):
        return start([remote(src, dst, cs.at[k], cr.at[k], cpeer)])

    barrier = pltpu.get_barrier_semaphore()
    peers = [zpeer(d) for d in zd] + [ypeer(d) for d in yd] + [xpeer(d) for d in xd] + [cpeer]
    for peer in peers:
        pl.semaphore_signal(barrier, inc=1, device_id=peer, device_id_type=MESH)

    iz_s[0] = ids_in[...]
    iz[z] = ids_in[...]
    ends = jnp.int32(0)
    seg_row = jnp.zeros((8, T), jnp.int32)
    seg_col = jnp.zeros((T, T), jnp.int32)
    row_t, col_t = iota((8, T), 1), iota((T, T), 0)
    for k in range(SEQS):
        ends = ends + lens[0, k]
        seg_row = seg_row + (row_t >= ends).astype(jnp.int32)
        seg_col = seg_col + (col_t >= ends).astype(jnp.int32)
    same = (seg_col == seg_row[0:1, :]) & (col_t >= iota((T, T), 1))
    slot = slots_in[...]
    mapped = (((slot >> lcap) & (ny - 1)) << lyb) + ((slot >> lzb) << lcap) + (slot & (cap - 1))
    eh = (col_t == mapped).astype(F32).astype(BF16)
    row_i, lane_i = iota((T, T), 0), iota((T, T), 1)
    to_y = (((row_i >> lcap) & (nz - 1)) << lzb) + ((row_i >> lyb) << lcap) + (row_i & (cap - 1))
    perm_zy = (lane_i == to_y).astype(F32).astype(BF16)
    to_z = (((row_i >> lcap) & (ny - 1)) << lyb) + ((row_i >> lzb) << lcap) + (row_i & (cap - 1))
    perm_yz = (lane_i == to_z).astype(F32).astype(BF16)

    pl.semaphore_wait(barrier, len(peers))

    got = along_z(0, lambda t, d: iz_s.at[0], lambda d: iz.at[z])
    arrive(got)
    lane8 = iota((8, T), 1)
    total = jnp.zeros((8, T), jnp.int32)
    for s in range(nz):
        row = jnp.broadcast_to(iz[s], (8, T))
        row = jnp.where((lane8 >> lzb) == z, row, 0)
        total = total + pltpu.roll(row, lax.rem((s - z) * zb + T, T), 1)
    iy[y] = total[0:1, :]
    got = along_y(0, lambda t, d: iy.at[y], lambda d: iy.at[y])
    arrive(got)
    total = jnp.zeros((8, T), jnp.int32)
    for s in range(ny):
        row = jnp.broadcast_to(iy[s], (8, T))
        row = jnp.where(((lane8 >> lcap) & (ny - 1)) == y, row, 0)
        total = total + pltpu.roll(row, lax.rem((s - y) * cap + T, T), 1)
    wanted[...] = total.astype(F32)
    rows_dev = table_in.shape[0]
    oht[...] = (iota((rows_dev, T), 0) == total[0:1, :]).astype(F32).astype(BF16)

    found = tn(oht[...], table_in[...].astype(BF16)).astype(BF16)
    a_s[...] = found.reshape(nz, zb, E)
    b_r[z] = a_s[z]
    got = along_z(1, lambda t, d: a_s.at[t], lambda d: b_r.at[z])
    pairs = tn(oht[...], oht[...])
    earlier = jnp.sum(jnp.where(lane_i < row_i, pairs, 0.0), axis=1, keepdims=True)
    first = jnp.where(earlier < 0.5, 1.0, 0.0)
    pairs = pairs.astype(BF16)
    state = state_in[...]
    flat = jnp.concatenate([state[k : k + 1, :] for k in range(rows_dev // T)], axis=1)
    high = flat.astype(BF16)
    rest = flat - high.astype(F32)
    mid = rest.astype(BF16)
    low = (rest - mid.astype(F32)).astype(BF16)
    three = jnp.concatenate(
        [jnp.broadcast_to(t, (16, rows_dev)) for t in (high, mid, low)], axis=0
    )
    at_rows = nn(three, oht[...])
    at_row = at_rows[0:1] + at_rows[16:17] + at_rows[32:33]
    diagonal = row_i == lane_i
    at_col = jnp.sum(jnp.where(diagonal, at_row, 0.0), axis=1, keepdims=True)
    arrive(got)
    turned = nn(perm_zy, b_r[...].reshape(T, E)).astype(BF16)
    c_s[...] = turned.reshape(ny, yb, E)
    d_r[y] = c_s[y]
    got = along_y(1, lambda t, d: c_s.at[t], lambda d: d_r.at[y])
    arrive(got)
    slot_rows = d_r[...].reshape(T, E)
    embedded = tn(eh, slot_rows)

    cot = cot_in[...]
    dx, normed, dpre, gated, dng, dog = layer(
        embedded, cot, w_in, wout_in, ng_in[...], og_in[...], same
    )

    dx_high, dx_low = split2(dx)
    slot_grad = (nn(eh, dx_high) + nn(eh, dx_low)).astype(BF16)
    e_s[...] = slot_grad.reshape(ny, yb, E)
    e_r[y] = e_s[y]
    got_grad = along_y(2, lambda t, d: e_s.at[t], lambda d: e_r.at[y])

    half = wacc.shape[3:][1]
    shape = wacc.shape[1:]
    wacc[0] = tn(normed, dpre[:, :half]).reshape(shape)
    dwout = tn(gated, cot)
    wacc[1] = jnp.concatenate([tn(normed, dpre[:, half:]), dwout], axis=1).reshape(shape)
    w1_s[...] = wacc[other].astype(BF16)
    got_w = across(0, w1_s, w1_r)
    ga_c[c] = jnp.concatenate([dng, dog, jnp.zeros((6, E), F32)], axis=0)
    got_ga = across(1, ga_c.at[c], ga_c.at[c])

    arrive(got_grad)
    turned = nn(perm_yz, e_r[...].reshape(T, E)).astype(BF16)
    f_s[...] = turned.reshape(nz, zb, E)
    g_r[z] = f_s[z]
    got_grad = along_z(2, lambda t, d: f_s.at[t], lambda d: g_r.at[z])

    arrive(got_w)
    acc2[...] = wacc[c] + w1_r[...].astype(F32)
    w2_s[...] = acc2[...].astype(BF16)
    got_w = along_x(0, lambda t, d: w2_s.at[t], lambda d: w2_r.at[d - 1])
    arrive(got_ga)
    ga_x[x] = ga_c[0] + ga_c[1]
    got_ga = along_x(1, lambda t, d: ga_x.at[x], lambda d: ga_x.at[x])

    arrive(got_grad)
    sums = nn(pairs, g_r[...].reshape(T, E))
    square = lane_mean(sums * sums)
    scale = (-LEARN_RATE) * first * lax.rsqrt(at_col + square + EPSILON)
    dall[rep] = (sums * scale).astype(BF16)
    square_row = jnp.sum(jnp.where(diagonal, square * first, 0.0), axis=0, keepdims=True)
    mall[rep] = jnp.concatenate([wanted[0:1, :], square_row, jnp.zeros((6, T), F32)], axis=0)
    got_m = along_x(3, lambda t, d: mall.at[rep], lambda d: mall.at[rep])
    got_m_c = across(2, mall.at[rep], mall.at[rep])
    got_d = along_x(2, lambda t, d: dall.at[rep], lambda d: dall.at[rep])
    got_d_c = across(3, dall.at[rep], dall.at[rep])

    arrive(got_w)
    acc3 = acc2[x]
    for d in range(nx - 1):
        acc3 = acc3 + w2_r[d].astype(F32)
    wacc[0, 0] = acc3
    w3_s[...] = acc3.astype(BF16)
    got_w = along_z(3, lambda t, d: w3_s.at[t], lambda d: w3_r.at[d - 1])
    arrive(got_ga)
    gsum = ga_x[0]
    for k in range(1, nx):
        gsum = gsum + ga_x[k]
    ga_z[z] = gsum
    got_ga = along_z(4, lambda t, d: ga_z.at[z], lambda d: ga_z.at[z])

    forwards = []
    arrive(got_m)
    arrive(got_d)
    for d in range(1, nx):
        source = lax.rem(x + nx - d, nx) * 2 + c
        forwards += across(4 + 2 * d, mall.at[source], mall.at[source])
        forwards += across(5 + 2 * d, dall.at[source], dall.at[source])

    arrive(got_w)
    acc4 = wacc[0, 0, z]
    for d in range(nz - 1):
        acc4 = acc4 + w3_r[d].astype(F32)
    w4[y] = acc4.astype(BF16)
    got_w = along_y(3, lambda t, d: w4.at[y], lambda d: w4.at[y])
    arrive(got_ga)
    gsum = ga_z[0]
    for k in range(1, nz):
        gsum = gsum + ga_z[k]
    ga_y[y] = gsum
    got_ga = along_y(4, lambda t, d: ga_y.at[y], lambda d: ga_y.at[y])
    arrive(got_m_c)
    arrive(got_d_c)
    arrive(forwards)

    arrive(got_w)
    scale = 1.0 / math.sqrt(T * nz * ny * nx * 2)
    acc5 = w4[0].astype(F32)
    for k in range(1, ny):
        acc5 = acc5 + w4[k].astype(F32)
    fin[c, x, z] = (acc5 * scale).astype(BF16)
    got_w = along_z(5, lambda t, d: fin.at[c, x, z], lambda d: fin.at[c, x, z])

    reps = 2 * nx
    squares = jnp.concatenate([mall[k][1:2, :] for k in range(reps)], axis=1)
    sq_high, sq_low = split2(squares)
    both = jnp.concatenate([jnp.broadcast_to(t, (16, reps * T)) for t in (sq_high, sq_low)], axis=0)
    asked = jnp.concatenate([mall[k][0:1, :] for k in range(reps)], axis=1)
    changes = dall[...].reshape(reps * T, E)
    for block in range(rows_dev // T):
        row_id = (iota((T, reps * T), 0) + block * T).astype(F32)
        hot = (row_id == asked).astype(F32).astype(BF16)
        rows_out[block * T : (block + 1) * T, :] = nn(hot, changes)
        add = nt(both, hot)
        state_out[block : block + 1, :] = state[block : block + 1, :] + (add[0:1] + add[16:17]) * (1.0 / reps)

    arrive(got_w)
    got_w = along_x(4, lambda t, d: fin.at[c, x], lambda d: fin.at[c, x])
    arrive(got_ga)
    gsum = ga_y[0]
    for k in range(1, ny):
        gsum = gsum + ga_y[k]
    gains_out[...] = gsum * scale
    arrive(got_w)
    got_w = across(4, fin.at[c], fin.at[c])
    arrive(got_w)
    fin_out[...] = fin[...]
    for copy in pending:
        copy.wait_send()


def on_device(nz, ny, nx, request_rows, token_slot, seq_lengths, cotangent, table_slab,
              adagrad_state, w_uvqk, w_out, norm_gain, out_gain):
    rows_dev = table_slab.shape[0]
    cap = T // (nz * ny)
    zb, yb = T // nz, T // ny
    chunk = (E // (nx * nz), 640)
    vmem = pl.BlockSpec(memory_space=pltpu.VMEM)
    smem = pl.BlockSpec(memory_space=pltpu.SMEM)
    reps = 2 * nx
    dma = pltpu.SemaphoreType.DMA
    V = pltpu.VMEM
    rows, state, fin, gains = pl.pallas_call(
        functools.partial(step_kernel, nz, ny, nx),
        out_shape=(
            jax.ShapeDtypeStruct((rows_dev, E), F32),
            jax.ShapeDtypeStruct((rows_dev // T, T), F32),
            jax.ShapeDtypeStruct((2, nx, nz, *chunk), BF16),
            jax.ShapeDtypeStruct((8, E), F32),
        ),
        in_specs=[smem] + [vmem] * 9,
        out_specs=(vmem,) * 4,
        scratch_shapes=[
            V((1, 1, T), jnp.int32), V((nz, 1, T), jnp.int32), V((ny, 1, T), jnp.int32),
            V((nz, zb, E), BF16), V((nz, zb, E), BF16), V((ny, yb, E), BF16), V((ny, yb, E), BF16),
            V((ny, yb, E), BF16), V((ny, yb, E), BF16), V((nz, zb, E), BF16), V((nz, zb, E), BF16),
            V((rows_dev, T), BF16), V((8, T), F32),
            V((reps, T, E), BF16), V((reps, 8, T), F32),
            V((2, nx, nz, *chunk), F32),
            V((nx, nz, *chunk), BF16), V((nx, nz, *chunk), BF16),
            V((nx, nz, *chunk), F32),
            V((nx, nz, *chunk), BF16), V((nx - 1, nz, *chunk), BF16),
            V((nz, *chunk), BF16), V((nz - 1, *chunk), BF16),
            V((ny, *chunk), BF16),
            V((2, nx, nz, *chunk), BF16),
            V((2, 8, E), F32), V((nx, 8, E), F32), V((nz, 8, E), F32), V((ny, 8, E), F32),
            dma((6, nz)), dma((6, nz)), dma((5, ny)), dma((5, ny)),
            dma((5, nx)), dma((5, nx)), dma((6 + 2 * nx,)), dma((6 + 2 * nx,)),
        ],
        compiler_params=pltpu.CompilerParams(collective_id=0, has_side_effects=True),
        name="step",
    )(
        seq_lengths.reshape(1, SEQS),
        request_rows.reshape(1, T),
        token_slot,
        cotangent[0],
        table_slab,
        adagrad_state.reshape(rows_dev // T, T),
        w_uvqk,
        w_out,
        norm_gain.reshape(1, E),
        out_gain.reshape(1, E),
    )
    halves = fin.reshape(2, E, 640).astype(F32)
    return (
        rows * (1.0 / reps),
        state.reshape(rows_dev),
        jnp.concatenate([halves[0], halves[1, :, :384]], axis=1),
        halves[1, :, 384:],
        gains[:2],
    )


def solution(mesh):
    shards, reps = mesh.shape["shard"], mesh.shape["replica"]
    side = math.isqrt(shards)
    return jax.shard_map(
        functools.partial(on_device, side, shards // side, reps // 2),
        mesh=mesh,
        in_specs=(
            P("replica", "shard", None),
            P("replica", "shard"),
            P("replica", "shard", None),
            P("replica", "shard", None),
            P("shard", None),
            P("shard"),
            P(),
            P(),
            P(),
            P(),
        ),
        out_specs=(P("shard", None), P("shard"), P(), P(), P()),
        check_vma=False,
    )
```

```python
import functools
import math

import jax
import jax.numpy as jnp
from jax import lax
from jax.experimental import pallas as pl
from jax.experimental.pallas import tpu as pltpu
from jax.sharding import PartitionSpec as P

HEADS = 4
MAXLEN = 48
SEQS = 8
EPSILON = 1e-08
LEARN_RATE = 0.5
E = 256
T = 128
F32 = jnp.float32
BF16 = jnp.bfloat16
MESH = pl.DeviceIdType.MESH


def far_first(n):
    return sorted(range(1, n), key=lambda d: -min(d, n - d))


def nn(a, b):
    return lax.dot_general(a, b, (((1,), (0,)), ((), ())), preferred_element_type=F32)


def nt(a, b):
    return lax.dot_general(a, b, (((1,), (1,)), ((), ())), preferred_element_type=F32)


def tn(a, b):
    return lax.dot_general(a, b, (((0,), (0,)), ((), ())), preferred_element_type=F32)


def iota(shape, dim):
    return lax.broadcasted_iota(jnp.int32, shape, dim)


def lane_mean(x):
    return jnp.sum(x, axis=1, keepdims=True) * (1.0 / x.shape[1])


def split2(x):
    high = x.astype(BF16)
    return high, (x - high.astype(F32)).astype(BF16)


def layer(x, cot, w_ref, wout_ref, ng, og, same):
    center = x - lane_mean(x)
    rstd = lax.rsqrt(lane_mean(center * center) + 1e-05)
    xhat = center * rstd
    normed = (xhat * ng).astype(BF16)
    pre = nn(normed, w_ref[...])
    sig = lax.logistic(pre)
    proj = pre * sig
    dsilu = sig * (1.0 + pre * (1.0 - sig))
    u = proj[:, :E]
    low = iota((T, 128), 1) < 64
    zero = jnp.zeros((T, 128), BF16)
    pairs, att = [], []
    for p in range(2):
        at = p * 128
        vp = proj[:, E + at : E + at + 128].astype(BF16)
        qp = proj[:, 2 * E + at : 2 * E + at + 128].astype(BF16)
        kp = proj[:, 3 * E + at : 3 * E + at + 128].astype(BF16)
        heads, total = [], None
        for h in range(2):
            mine = low if h == 0 else jnp.logical_not(low)
            qh, kh = jnp.where(mine, qp, zero), jnp.where(mine, kp, zero)
            s = nt(qh, kp) * 0.125
            sg = lax.logistic(s)
            weights = jnp.where(same, s * sg * (1.0 / MAXLEN), 0.0).astype(BF16)
            slope = jnp.where(same, sg * (1.0 + s * (1.0 - sg)) * (0.125 / MAXLEN), 0.0)
            part = nn(weights, jnp.where(mine, vp, zero))
            total = part if total is None else total + part
            heads.append((mine, qh, kh, weights, slope))
        pairs.append((vp, heads))
        att.append(total)
    attended = jnp.concatenate(att, axis=1)
    center2 = attended - lane_mean(attended)
    rstd2 = lax.rsqrt(lane_mean(center2 * center2) + 1e-05)
    ahat = center2 * rstd2
    gated = (ahat * og * u).astype(BF16)
    dgated = nt(cot, wout_ref[...]).astype(BF16).astype(F32)
    au = ahat * u
    dog = jnp.sum(dgated * au, axis=0, keepdims=True)
    dgo = dgated * og
    du = dgo * ahat
    dahat = dgo * u
    datt = rstd2 * (dahat - lane_mean(dahat) - ahat * lane_mean(dahat * ahat))
    datt = datt.astype(BF16)
    dvs, dqs, dks = [], [], []
    for p in range(2):
        vp, heads = pairs[p]
        dp = datt[:, p * 128 : p * 128 + 128]
        dv = dq = dk = None
        for mine, qh, kh, weights, slope in heads:
            dh = jnp.where(mine, dp, zero)
            dw = nt(dh, vp).astype(BF16).astype(F32)
            ds = (dw * slope).astype(BF16)
            a, b, c = tn(weights, dh), nn(ds, kh), tn(ds, qh)
            dv, dq, dk = (a, b, c) if dv is None else (dv + a, dq + b, dk + c)
        dvs.append(dv)
        dqs.append(dq)
        dks.append(dk)
    rounded = [t.astype(BF16).astype(F32) for t in (*dvs, *dqs, *dks)]
    dproj = jnp.concatenate([du, *rounded], axis=1)
    dpre = (dproj * dsilu).astype(BF16)
    dnormed = nt(dpre, w_ref[...]).astype(BF16).astype(F32)
    dng = jnp.sum(dnormed * xhat, axis=0, keepdims=True)
    dxhat = dnormed * ng
    dx = rstd * (dxhat - lane_mean(dxhat) - xhat * lane_mean(dxhat * xhat)) + cot.astype(F32)
    return dx, normed, dpre, gated, dng, dog


def step_kernel(
    nz, ny, nx,
    lens_in, ids_in, slots_in, cot_in, table_in, state_in, w_in, wout_in, ng_in, og_in,
    rows_out, state_out, fin_out, gains_out,
    lens, ids, slots, cot_v, table, state_v, w, wout, ng, og,
    iz, iy, a_s, d_r, e_s, g_r, hot_rows, table_b,
    dall, mall, wacc, w1_s, w1_r, acc2, w2_s, w2_r, w3_s, w3_r, w4, fin,
    ga_c, ga_x, ga_z, ga_y,
    ls, zs, zr, ys, yr, xs, xr, cs, cr, rs_s, rs_r, p1s, p1r, p2s, p2r, gxs, gxr, gcs, gcr,
):
    shards, reps = nz * ny, 2 * nx
    cap = T // shards
    zb = T // nz
    lcap, lzb = int(math.log2(cap)), int(math.log2(zb))
    rows_dev = table.shape[0]
    shard, rep = lax.axis_index("shard"), lax.axis_index("replica")
    z, y = shard // ny, lax.rem(shard, ny)
    x, c = rep // 2, lax.rem(rep, 2)
    other = 1 - c
    zat = lambda d: lax.rem(z + d, nz)
    yat = lambda d: lax.rem(y + d, ny)
    xat = lambda d: lax.rem(x + d, nx)
    zpeer = lambda d: {"shard": zat(d) * ny + y}
    ypeer = lambda d: {"shard": z * ny + yat(d)}
    xpeer = lambda d: {"replica": xat(d) * 2 + c}
    cpeer = {"replica": x * 2 + other}
    zd, yd, xd = far_first(nz), far_first(ny), far_first(nx)
    hops = lambda d, n: min(d, n - d)
    plane = [(a, b) for a in range(nz) for b in range(ny) if a or b]
    plane.sort(key=lambda d: -(hops(d[0], nz) + hops(d[1], ny)))

    def remote(src, dst, ssem, rsem, peer):
        return pltpu.make_async_remote_copy(
            src_ref=src, dst_ref=dst, send_sem=ssem, recv_sem=rsem,
            device_id=peer, device_id_type=MESH,
        )

    pending = []

    def start(copies):
        for copy in copies:
            copy.start()
        pending.extend(copies)
        return copies

    def arrive(copies):
        for copy in copies:
            copy.wait_recv()

    def along_z(k, src, dst):
        return start([remote(src(d), dst(d), zs.at[k, d], zr.at[k, d], zpeer(d)) for d in zd])

    def along_y(k, src, dst):
        return start([remote(src(d), dst(d), ys.at[k, d], yr.at[k, d], ypeer(d)) for d in yd])

    def along_x(k, src, dst):
        return start([remote(src(d), dst(d), xs.at[k, d], xr.at[k, d], xpeer(d)) for d in xd])

    def across(k, src, dst):
        return start([remote(src, dst, cs.at[k], cr.at[k], cpeer)])

    def to_plane(k, src, dst):
        copies = []
        for a, b in plane:
            target = zat(a) * ny + yat(b)
            e = a * ny + b
            copies.append(
                remote(src.at[target], dst.at[shard], rs_s.at[k, e], rs_r.at[k, e], {"shard": target})
            )
        return start(copies)

    barrier = pltpu.get_barrier_semaphore()
    peers = [zpeer(d) for d in zd] + [ypeer(d) for d in yd] + [xpeer(d) for d in xd] + [cpeer]
    for peer in peers:
        pl.semaphore_signal(barrier, inc=1, device_id=peer, device_id_type=MESH)
    sources = (ids_in, lens_in, slots_in, state_in, ng_in, og_in, table_in, cot_in, w_in, wout_in)
    targets = (ids, lens, slots, state_v, ng, og, table, cot_v, w, wout)
    loads = [
        pltpu.make_async_copy(src, dst, ls.at[k]) for k, (src, dst) in enumerate(zip(sources, targets))
    ]
    for load in loads:
        load.start()

    for load in loads[:6]:
        load.wait()
    iz[z] = ids[0]
    row_i, lane_i = iota((T, T), 0), iota((T, T), 1)
    diagonal = row_i == lane_i
    ends = jnp.int32(0)
    seg_row = jnp.zeros((8, T), jnp.int32)
    seg_col = jnp.zeros((T, T), jnp.int32)
    row_t = iota((8, T), 1)
    for k in range(SEQS):
        ends = ends + lens[0, k]
        seg_row = seg_row + (row_t >= ends).astype(jnp.int32)
        seg_col = seg_col + (row_i >= ends).astype(jnp.int32)
    same = (seg_col == seg_row[0:1, :]) & (row_i >= lane_i)
    slot = slots[...].astype(F32)
    slot_col = jnp.sum(jnp.where(diagonal, slot, 0.0), axis=1, keepdims=True)
    of_slot = (row_i.astype(F32) == slot).astype(F32).astype(BF16)
    of_token = (lane_i.astype(F32) == slot_col).astype(F32).astype(BF16)

    pl.semaphore_wait(barrier, len(peers))

    got = along_z(0, lambda d: ids.at[0], lambda d: iz.at[z])
    loads[6].wait()
    table_b[...] = table[...].astype(BF16)
    arrive(got)
    total = jnp.zeros((8, T), jnp.int32)
    for s in range(nz):
        row = jnp.broadcast_to(iz[s], (8, T))
        row = jnp.where((row_t >> lzb) == z, row, 0)
        total = total + pltpu.roll(row, lax.rem((s - z) * zb + T, T), 1)
    iy[y] = total[0:1, :]
    got = along_y(0, lambda d: iy.at[y], lambda d: iy.at[y])
    for load in loads[7:]:
        load.wait()
    arrive(got)
    total = jnp.zeros((8, T), jnp.int32)
    for s in range(ny):
        row = jnp.broadcast_to(iy[s], (8, T))
        row = jnp.where(((row_t >> lcap) & (ny - 1)) == y, row, 0)
        total = total + pltpu.roll(row, lax.rem((s - y) * cap + T, T), 1)
    asked_row = total[0:1, :].astype(F32)
    asked_col = jnp.sum(jnp.where(diagonal, asked_row, 0.0), axis=1, keepdims=True)
    table_row = iota((1, rows_dev), 1).astype(F32)
    hot_rows[...] = (table_row == asked_col).astype(F32).astype(BF16)

    found = nn(hot_rows[...], table_b[...]).astype(BF16)
    a_s[...] = found.reshape(shards, cap, E)
    d_r[shard] = a_s[shard]
    got = to_plane(0, a_s, d_r)
    hot = hot_rows[...]
    pairs = nt(hot, hot)
    earlier = jnp.sum(jnp.where(lane_i < row_i, pairs, 0.0), axis=1, keepdims=True)
    first = jnp.where(earlier < 0.5, 1.0, 0.0)
    pairs = pairs.astype(BF16)
    state = state_v[...]
    flat = jnp.concatenate([state[k : k + 1, :] for k in range(rows_dev // T)], axis=1)
    high = flat.astype(BF16)
    rest = flat - high.astype(F32)
    mid = rest.astype(BF16)
    low = (rest - mid.astype(F32)).astype(BF16)
    three = jnp.concatenate(
        [jnp.broadcast_to(t, (16, rows_dev)) for t in (high, mid, low)], axis=0
    )
    at_rows = nt(three, hot)
    at_row = at_rows[0:1] + at_rows[16:17] + at_rows[32:33]
    at_col = jnp.sum(jnp.where(diagonal, at_row, 0.0), axis=1, keepdims=True)
    arrive(got)
    embedded = nn(of_token, d_r[...].reshape(T, E))
    cot = cot_v[...]
    dx, normed, dpre, gated, dng, dog = layer(
        embedded, cot, w, wout, ng[...], og[...], same
    )

    dx_high, dx_low = split2(dx)
    slot_grad = (nn(of_slot, dx_high) + nn(of_slot, dx_low)).astype(BF16)
    e_s[...] = slot_grad.reshape(shards, cap, E)
    g_r[shard] = e_s[shard]
    got_grad = to_plane(1, e_s, g_r)

    half = wacc.shape[4]
    shape = wacc.shape[1:]
    wacc[0] = tn(normed, dpre[:, :half]).reshape(shape)
    dwout = tn(gated, cot)
    wacc[1] = jnp.concatenate([tn(normed, dpre[:, half:]), dwout], axis=1).reshape(shape)
    w1_s[...] = wacc[other].astype(BF16)
    chunks = zd + [0]
    hop = {}
    for d in chunks:
        hop[d] = start([remote(w1_s.at[zat(d)], w1_r.at[zat(d)], p1s.at[d], p1r.at[d], cpeer)])
    ga_c[c] = jnp.concatenate([dng, dog, jnp.zeros((6, E), F32)], axis=0)
    got_ga = across(0, ga_c.at[c], ga_c.at[c])
    for d in chunks:
        arrive(hop[d])
        summed = wacc[c, zat(d)] + w1_r[zat(d)].astype(F32)
        acc2[zat(d)] = summed
        w2_s[zat(d)] = summed.astype(BF16)
        hop[d] = start([
            remote(w2_s.at[zat(d), xat(e)], w2_r.at[zat(d), e - 1], p2s.at[d, e], p2r.at[d, e], xpeer(e))
            for e in xd
        ])
    arrive(got_ga)
    ga_x[x] = ga_c[0] + ga_c[1]
    got_ga = along_x(0, lambda d: ga_x.at[x], lambda d: ga_x.at[x])
    got_w = []
    for d in chunks:
        arrive(hop[d])
        acc3 = acc2[zat(d), x]
        for e in range(nx - 1):
            acc3 = acc3 + w2_r[zat(d), e].astype(F32)
        if d:
            w3_s[d - 1] = acc3.astype(BF16)
            got_w += start([remote(w3_s.at[d - 1], w3_r.at[d - 1], zs.at[1, d], zr.at[1, d], zpeer(d))])
    arrive(got_ga)
    gsum = ga_x[0]
    for k in range(1, nx):
        gsum = gsum + ga_x[k]
    ga_z[z] = gsum
    got_ga = along_z(2, lambda d: ga_z.at[z], lambda d: ga_z.at[z])

    arrive(got_grad)
    sums = nn(pairs, g_r[...].reshape(T, E))
    square = lane_mean(sums * sums)
    scale = (-LEARN_RATE) * first * lax.rsqrt(at_col + square + EPSILON)
    dall[rep] = (sums * scale).astype(BF16)
    square_row = jnp.sum(jnp.where(diagonal, square * first, 0.0), axis=0, keepdims=True)
    mall[rep] = jnp.concatenate([asked_row, square_row, jnp.zeros((6, T), F32)], axis=0)
    got_d = along_x(1, lambda d: dall.at[rep], lambda d: dall.at[rep])
    got_m = along_x(2, lambda d: mall.at[rep], lambda d: mall.at[rep])
    forwards = across(1, dall.at[rep], dall.at[rep]) + across(2, mall.at[rep], mall.at[rep])

    arrive(got_w)
    for d in range(1, nz):
        acc3 = acc3 + w3_r[d - 1].astype(F32)
    w4[y] = acc3.astype(BF16)
    got_w = along_y(1, lambda d: w4.at[y], lambda d: w4.at[y])
    arrive(got_ga)
    gsum = ga_z[0]
    for k in range(1, nz):
        gsum = gsum + ga_z[k]
    ga_y[y] = gsum
    got_ga = along_y(2, lambda d: ga_y.at[y], lambda d: ga_y.at[y])

    arrive(got_d)
    arrive(got_m)
    for d in range(1, nx):
        source = xat(nx - d) * 2 + c
        forwards += across(1 + 2 * d, dall.at[source], dall.at[source])
        forwards += across(2 + 2 * d, mall.at[source], mall.at[source])

    arrive(got_w)
    scale = 1.0 / math.sqrt(T * shards * reps)
    acc5 = w4[0].astype(F32)
    for k in range(1, ny):
        acc5 = acc5 + w4[k].astype(F32)
    fin[c, z, x] = (acc5 * scale).astype(BF16)
    from_z = dict(zip(zd, along_z(3, lambda d: fin.at[c, z, x], lambda d: fin.at[c, z, x])))
    near = [0] + zd[::-1]

    def pass_on(d):
        at = zat(nz - d) if d else z
        chunk = fin.at[c, at, x]
        to_x = start([remote(chunk, chunk, gxs.at[d, e], gxr.at[d, e], xpeer(e)) for e in xd])
        to_c = start([remote(chunk, chunk, gcs.at[d, 0], gcr.at[d, 0], cpeer)])
        return to_x, to_c

    from_x, from_c = {}, []
    from_x[0], sent = pass_on(0)
    from_c += sent

    arrive(forwards)
    squares = jnp.concatenate([mall[k][1:2, :] for k in range(reps)], axis=1)
    sq_high, sq_low = split2(squares)
    both = jnp.concatenate([jnp.broadcast_to(t, (16, reps * T)) for t in (sq_high, sq_low)], axis=0)
    asked = jnp.concatenate([mall[k][0:1, :] for k in range(reps)], axis=1)
    changes = dall[...].reshape(reps * T, E)
    share = 1.0 / reps
    for block in range(rows_dev // T):
        row_id = (iota((T, 1), 0) + block * T).astype(F32)
        hot = (row_id == asked).astype(F32).astype(BF16)
        rows_out[block * T : (block + 1) * T, :] = nn(hot, changes) * share
        add = nt(both, hot)
        state_out[block : block + 1, :] = state[block : block + 1, :] + (add[0:1] + add[16:17]) * share

    for d in near[1:]:
        arrive([from_z[d]])
        from_x[d], sent = pass_on(d)
        from_c += sent
    arrive(got_ga)
    gsum = ga_y[0]
    for k in range(1, ny):
        gsum = gsum + ga_y[k]
    gains_out[...] = gsum * scale
    for d in near:
        at = zat(nz - d) if d else z
        for e, copy in zip(xd, from_x[d]):
            arrive([copy])
            chunk = fin.at[c, at, xat(nx - e)]
            from_c += start([remote(chunk, chunk, gcs.at[d, e], gcr.at[d, e], cpeer)])
    arrive(from_c)
    fin_out[...] = fin[...]
    for copy in pending:
        copy.wait_send()


def write_kernel(rows, state, fin, gains, rows_o, state_o, uvqk_o, wout_o, gains_o, uvqk, wout, sem):
    first = pltpu.make_async_copy(rows, rows_o, sem.at[0])
    first.start()
    width = fin.shape[2]
    uvqk[:, :width] = fin[0].astype(F32)
    uvqk[:, width:] = fin[1, :, : uvqk.shape[1] - width].astype(F32)
    second = pltpu.make_async_copy(uvqk, uvqk_o, sem.at[1])
    second.start()
    wout[...] = fin[1, :, uvqk.shape[1] - width :].astype(F32)
    third = pltpu.make_async_copy(wout, wout_o, sem.at[2])
    third.start()
    state_o[...] = state[...]
    gains_o[...] = gains[0:2, :]
    first.wait()
    second.wait()
    third.wait()


def on_device(nz, ny, nx, request_rows, token_slot, seq_lengths, cotangent, table_slab,
              adagrad_state, w_uvqk, w_out, norm_gain, out_gain):
    rows_dev = table_slab.shape[0]
    shards, reps = nz * ny, 2 * nx
    cap = T // shards
    chunk = (E // (nx * nz), 640)
    vmem = pl.BlockSpec(memory_space=pltpu.VMEM)
    hbm = pl.BlockSpec(memory_space=pltpu.HBM)
    dma = pltpu.SemaphoreType.DMA
    V = pltpu.VMEM
    I32 = jnp.int32
    rows, state, fin, gains = pl.pallas_call(
        functools.partial(step_kernel, nz, ny, nx),
        out_shape=(
            jax.ShapeDtypeStruct((rows_dev, E), F32),
            jax.ShapeDtypeStruct((rows_dev // T, T), F32),
            jax.ShapeDtypeStruct((2, nz, nx, *chunk), BF16),
            jax.ShapeDtypeStruct((8, E), F32),
        ),
        in_specs=[hbm] * 10,
        out_specs=(vmem,) * 4,
        scratch_shapes=[
            pltpu.SMEM((1, SEQS), I32), V((1, 1, T), I32), V((1, T), I32), V((T, E), BF16),
            V((rows_dev, E), F32), V((rows_dev // T, T), F32), V((E, 4 * E), BF16), V((E, E), BF16),
            V((1, E), F32), V((1, E), F32),
            V((nz, 1, T), I32), V((ny, 1, T), I32),
            V((shards, cap, E), BF16), V((shards, cap, E), BF16),
            V((shards, cap, E), BF16), V((shards, cap, E), BF16),
            V((T, rows_dev), BF16), V((rows_dev, E), BF16),
            V((reps, T, E), BF16), V((reps, 8, T), F32),
            V((2, nz, nx, *chunk), F32),
            V((nz, nx, *chunk), BF16), V((nz, nx, *chunk), BF16),
            V((nz, nx, *chunk), F32),
            V((nz, nx, *chunk), BF16), V((nz, nx - 1, *chunk), BF16),
            V((nz - 1, *chunk), BF16), V((nz - 1, *chunk), BF16),
            V((ny, *chunk), BF16),
            V((2, nz, nx, *chunk), BF16),
            V((2, 8, E), F32), V((nx, 8, E), F32), V((nz, 8, E), F32), V((ny, 8, E), F32),
            dma((10,)),
            dma((4, nz)), dma((4, nz)), dma((3, ny)), dma((3, ny)),
            dma((3, nx)), dma((3, nx)), dma((1 + 2 * nx,)), dma((1 + 2 * nx,)),
            dma((2, shards)), dma((2, shards)),
            dma((nz,)), dma((nz,)), dma((nz, nx)), dma((nz, nx)),
            dma((nz, nx)), dma((nz, nx)), dma((nz, nx)), dma((nz, nx)),
        ],
        compiler_params=pltpu.CompilerParams(
            collective_id=0, has_side_effects=True, vmem_limit_bytes=24 << 20
        ),
        name="step",
    )(
        *(
            pltpu.with_memory_space_constraint(a, pltpu.HBM)
            for a in (
                seq_lengths.reshape(1, SEQS),
                request_rows.reshape(1, 1, T),
                token_slot,
                cotangent[0],
                table_slab,
                adagrad_state.reshape(rows_dev // T, T),
                w_uvqk,
                w_out,
                norm_gain.reshape(1, E),
                out_gain.reshape(1, E),
            )
        )
    )
    rows, state, uvqk, wout, gains = pl.pallas_call(
        write_kernel,
        out_shape=(
            jax.ShapeDtypeStruct((rows_dev, E), F32),
            jax.ShapeDtypeStruct((rows_dev // T, T), F32),
            jax.ShapeDtypeStruct((E, 4 * E), F32),
            jax.ShapeDtypeStruct((E, E), F32),
            jax.ShapeDtypeStruct((2, E), F32),
        ),
        in_specs=[vmem] * 4,
        out_specs=(hbm, vmem, hbm, hbm, vmem),
        scratch_shapes=[V((E, 4 * E), F32), V((E, E), F32), dma((3,))],
        compiler_params=pltpu.CompilerParams(vmem_limit_bytes=24 << 20),
        name="write",
    )(rows, state, fin.reshape(2, E, 640), gains)
    return rows, state.reshape(rows_dev), uvqk, wout, gains


def solution(mesh):
    shards, reps = mesh.shape["shard"], mesh.shape["replica"]
    side = math.isqrt(shards)
    return jax.shard_map(
        functools.partial(on_device, side, shards // side, reps // 2),
        mesh=mesh,
        in_specs=(
            P("replica", "shard", None),
            P("replica", "shard"),
            P("replica", "shard", None),
            P("replica", "shard", None),
            P("shard", None),
            P("shard"),
            P(),
            P(),
            P(),
            P(),
        ),
        out_specs=(P("shard", None), P("shard"), P(), P(), P()),
        check_vma=False,
    )
```

```python
import functools
import math

import jax
import jax.numpy as jnp
from jax import lax
from jax.experimental import pallas as pl
from jax.experimental.pallas import tpu as pltpu
from jax.sharding import PartitionSpec as P

HEADS = 4
MAXLEN = 48
SEQS = 8
EPSILON = 1e-08
LEARN_RATE = 0.5
E = 256
T = 128
F32 = jnp.float32
BF16 = jnp.bfloat16
MESH = pl.DeviceIdType.MESH


def far_first(n):
    return sorted(range(1, n), key=lambda d: -min(d, n - d))


def nn(a, b):
    return lax.dot_general(a, b, (((1,), (0,)), ((), ())), preferred_element_type=F32)


def nt(a, b):
    return lax.dot_general(a, b, (((1,), (1,)), ((), ())), preferred_element_type=F32)


def tn(a, b):
    return lax.dot_general(a, b, (((0,), (0,)), ((), ())), preferred_element_type=F32)


def iota(shape, dim):
    return lax.broadcasted_iota(jnp.int32, shape, dim)


def lane_mean(x):
    return jnp.sum(x, axis=1, keepdims=True) * (1.0 / x.shape[1])


def split2(x):
    high = x.astype(BF16)
    return high, (x - high.astype(F32)).astype(BF16)


def layer(x, cot, w_ref, wout_ref, ng, og, same):
    center = x - lane_mean(x)
    rstd = lax.rsqrt(lane_mean(center * center) + 1e-05)
    xhat = center * rstd
    normed = (xhat * ng).astype(BF16)
    pre = nn(normed, w_ref[...])
    sig = lax.logistic(pre)
    proj = pre * sig
    dsilu = sig * (1.0 + pre * (1.0 - sig))
    u = proj[:, :E]
    low = iota((T, 128), 1) < 64
    zero = jnp.zeros((T, 128), BF16)
    pairs, att = [], []
    for p in range(2):
        at = p * 128
        vp = proj[:, E + at : E + at + 128].astype(BF16)
        qp = proj[:, 2 * E + at : 2 * E + at + 128].astype(BF16)
        kp = proj[:, 3 * E + at : 3 * E + at + 128].astype(BF16)
        heads, total = [], None
        for h in range(2):
            mine = low if h == 0 else jnp.logical_not(low)
            qh, kh = jnp.where(mine, qp, zero), jnp.where(mine, kp, zero)
            s = nt(qh, kp) * 0.125
            sg = lax.logistic(s)
            weights = jnp.where(same, s * sg * (1.0 / MAXLEN), 0.0).astype(BF16)
            slope = jnp.where(same, sg * (1.0 + s * (1.0 - sg)) * (0.125 / MAXLEN), 0.0)
            part = nn(weights, jnp.where(mine, vp, zero))
            total = part if total is None else total + part
            heads.append((mine, qh, kh, weights, slope))
        pairs.append((vp, heads))
        att.append(total)
    attended = jnp.concatenate(att, axis=1)
    center2 = attended - lane_mean(attended)
    rstd2 = lax.rsqrt(lane_mean(center2 * center2) + 1e-05)
    ahat = center2 * rstd2
    gated = (ahat * og * u).astype(BF16)
    dgated = nt(cot, wout_ref[...]).astype(BF16).astype(F32)
    au = ahat * u
    dog = jnp.sum(dgated * au, axis=0, keepdims=True)
    dgo = dgated * og
    du = dgo * ahat
    dahat = dgo * u
    datt = rstd2 * (dahat - lane_mean(dahat) - ahat * lane_mean(dahat * ahat))
    datt = datt.astype(BF16)
    dvs, dqs, dks = [], [], []
    for p in range(2):
        vp, heads = pairs[p]
        dp = datt[:, p * 128 : p * 128 + 128]
        dv = dq = dk = None
        for mine, qh, kh, weights, slope in heads:
            dh = jnp.where(mine, dp, zero)
            dw = nt(dh, vp).astype(BF16).astype(F32)
            ds = (dw * slope).astype(BF16)
            a, b, c = tn(weights, dh), nn(ds, kh), tn(ds, qh)
            dv, dq, dk = (a, b, c) if dv is None else (dv + a, dq + b, dk + c)
        dvs.append(dv)
        dqs.append(dq)
        dks.append(dk)
    rounded = [t.astype(BF16).astype(F32) for t in (*dvs, *dqs, *dks)]
    dproj = jnp.concatenate([du, *rounded], axis=1)
    dpre = (dproj * dsilu).astype(BF16)
    dnormed = nt(dpre, w_ref[...]).astype(BF16).astype(F32)
    dng = jnp.sum(dnormed * xhat, axis=0, keepdims=True)
    dxhat = dnormed * ng
    dx = rstd * (dxhat - lane_mean(dxhat) - xhat * lane_mean(dxhat * xhat)) + cot.astype(F32)
    return dx, normed, dpre, gated, dng, dog


def step_kernel(
    nz, ny, nx,
    lens_in, ids_in, slots_in, cot_in, table_in, state_in, w_in, wout_in, ng_in, og_in,
    rows_out, state_out, fina_out, finb_out, gains_out,
    lens, ids, slots, cot_v, table, state_v, w, wout, ng, og,
    iz, iy, a_s, d_r, e_s, g_r, hot_rows, table_b, dall, mall,
    wacc_a, wacc_b, w1s_a, w1s_b, w1r_a, w1r_b, acc_a, acc_b, w2s_a, w2s_b, w2r_a, w2r_b,
    w3s_a, w3s_b, w3r_a, w3r_b, w4_a, w4_b,
    fin_a, fin_b, ga_c, ga_x, ga_z, ga_y,
    ls, zs, zr, ys, yr, xs, xr, cs, cr, rs_s, rs_r, p1s, p1r, p2s, p2r, p3s, p3r, p4s, p4r,
    as_, ar, bs, br, gas, gar, gbs, gbr, known,
):
    shards, reps = nz * ny, 2 * nx
    cap = T // shards
    zb = T // nz
    lcap, lzb = int(math.log2(cap)), int(math.log2(zb))
    rows_dev = table.shape[0]
    shard, rep = lax.axis_index("shard"), lax.axis_index("replica")
    z, y = shard // ny, lax.rem(shard, ny)
    x, c = rep // 2, lax.rem(rep, 2)
    other = 1 - c
    zat = lambda d: lax.rem(z + d, nz)
    yat = lambda d: lax.rem(y + d, ny)
    xat = lambda d: lax.rem(x + d, nx)
    zpeer = lambda d: {"shard": zat(d) * ny + y}
    ypeer = lambda d: {"shard": z * ny + yat(d)}
    xpeer = lambda d: {"replica": xat(d) * 2 + c}
    cpeer = {"replica": x * 2 + other}
    zd, yd, xd = far_first(nz), far_first(ny), far_first(nx)
    hops = lambda d, n: min(d, n - d)
    plane = [(a, b) for a in range(nz) for b in range(ny) if a or b]
    plane.sort(key=lambda d: -(hops(d[0], nz) + hops(d[1], ny)))
    n = nz
    box = [(a, b) for a in range(n) for b in range(nx) if a or b]
    box.sort(key=lambda d: -(hops(d[0], n) + hops(d[1], nx)))
    upos, vpos = z + c * (y - z), y + c * (z - y)
    uat = lambda d: lax.rem(upos + d, n)
    vat = lambda d: lax.rem(vpos + d, n)
    ushard = lambda d: zat((1 - c) * d) * ny + yat(c * d)
    vshard = lambda d: zat(c * d) * ny + yat((1 - c) * d)
    ux_at = lambda a, b: uat(a) * nx + xat(b)
    vx_at = lambda a, b: vat(a) * nx + xat(b)
    ux = lambda a, b: {"shard": ushard(a), "replica": xat(b) * 2 + c}
    vx = lambda a, b: {"shard": vshard(a), "replica": xat(b) * 2 + c}

    def remote(src, dst, ssem, rsem, peer):
        return pltpu.make_async_remote_copy(
            src_ref=src, dst_ref=dst, send_sem=ssem, recv_sem=rsem,
            device_id=peer, device_id_type=MESH,
        )

    pending = []

    def drain():
        for copy in pending:
            copy.wait_send()
        pending.clear()

    def start(copies):
        for copy in copies:
            copy.start()
        pending.extend(copies)
        return copies

    def arrive(copies):
        for copy in copies:
            copy.wait_recv()

    def along_z(k, src, dst):
        return start([remote(src(d), dst(d), zs.at[k, d], zr.at[k, d], zpeer(d)) for d in zd])

    def along_y(k, src, dst):
        return start([remote(src(d), dst(d), ys.at[k, d], yr.at[k, d], ypeer(d)) for d in yd])

    def along_x(k, src, dst):
        return start([remote(src(d), dst(d), xs.at[k, d], xr.at[k, d], xpeer(d)) for d in xd])

    def across(k, src, dst):
        return start([remote(src, dst, cs.at[k], cr.at[k], cpeer)])

    def to_plane(k, src, dst):
        copies = []
        for a, b in plane:
            target = zat(a) * ny + yat(b)
            e = a * ny + b
            copies.append(
                remote(src.at[target], dst.at[shard], rs_s.at[k, e], rs_r.at[k, e], {"shard": target})
            )
        return start(copies)

    barrier = pltpu.get_barrier_semaphore()
    peers = [zpeer(d) for d in zd] + [ypeer(d) for d in yd] + [xpeer(d) for d in xd] + [cpeer]
    for peer in peers:
        pl.semaphore_signal(barrier, inc=1, device_id=peer, device_id_type=MESH)
    sources = (ids_in, lens_in, slots_in, state_in, ng_in, og_in, table_in, cot_in, w_in, wout_in)
    targets = (ids, lens, slots, state_v, ng, og, table, cot_v, w, wout)
    loads = [
        pltpu.make_async_copy(src, dst, ls.at[k]) for k, (src, dst) in enumerate(zip(sources, targets))
    ]
    for load in loads:
        load.start()

    for load in loads[:6]:
        load.wait()
    iz[z] = ids[0]
    row_i, lane_i = iota((T, T), 0), iota((T, T), 1)
    diagonal = row_i == lane_i
    ends = jnp.int32(0)
    seg_row = jnp.zeros((8, T), jnp.int32)
    seg_col = jnp.zeros((T, T), jnp.int32)
    row_t = iota((8, T), 1)
    for k in range(SEQS):
        ends = ends + lens[0, k]
        seg_row = seg_row + (row_t >= ends).astype(jnp.int32)
        seg_col = seg_col + (row_i >= ends).astype(jnp.int32)
    same = (seg_col == seg_row[0:1, :]) & (row_i >= lane_i)
    slot = slots[...].astype(F32)
    slot_col = jnp.sum(jnp.where(diagonal, slot, 0.0), axis=1, keepdims=True)
    of_slot = (row_i.astype(F32) == slot).astype(F32).astype(BF16)
    of_token = (lane_i.astype(F32) == slot_col).astype(F32).astype(BF16)

    pl.semaphore_wait(barrier, len(peers))

    got = along_z(0, lambda d: ids.at[0], lambda d: iz.at[z])
    loads[6].wait()
    table_b[...] = table[...].astype(BF16)
    arrive(got)
    total = jnp.zeros((8, T), jnp.int32)
    for s in range(nz):
        row = jnp.broadcast_to(iz[s], (8, T))
        row = jnp.where((row_t >> lzb) == z, row, 0)
        total = total + pltpu.roll(row, lax.rem((s - z) * zb + T, T), 1)
    iy[y] = total[0:1, :]
    got = along_y(0, lambda d: iy.at[y], lambda d: iy.at[y])
    for load in loads[7:]:
        load.wait()
    arrive(got)
    total = jnp.zeros((8, T), jnp.int32)
    for s in range(ny):
        row = jnp.broadcast_to(iy[s], (8, T))
        row = jnp.where(((row_t >> lcap) & (ny - 1)) == y, row, 0)
        total = total + pltpu.roll(row, lax.rem((s - y) * cap + T, T), 1)
    asked_row = total[0:1, :].astype(F32)
    asked_col = jnp.sum(jnp.where(diagonal, asked_row, 0.0), axis=1, keepdims=True)
    table_row = iota((1, rows_dev), 1).astype(F32)
    hot_rows[...] = (table_row == asked_col).astype(F32).astype(BF16)

    found = nn(hot_rows[...], table_b[...]).astype(BF16)
    a_s[...] = found.reshape(shards, cap, E)
    d_r[shard] = a_s[shard]
    got = to_plane(0, a_s, d_r)
    hot = hot_rows[...]
    pairs = nt(hot, hot)
    earlier = jnp.sum(jnp.where(lane_i < row_i, pairs, 0.0), axis=1, keepdims=True)
    first = jnp.where(earlier < 0.5, 1.0, 0.0)
    pairs = pairs.astype(BF16)
    state = state_v[...]
    flat = jnp.concatenate([state[k : k + 1, :] for k in range(rows_dev // T)], axis=1)
    high = flat.astype(BF16)
    rest = flat - high.astype(F32)
    mid = rest.astype(BF16)
    low = (rest - mid.astype(F32)).astype(BF16)
    three = jnp.concatenate(
        [jnp.broadcast_to(t, (16, rows_dev)) for t in (high, mid, low)], axis=0
    )
    at_rows = nt(three, hot)
    at_row = at_rows[0:1] + at_rows[16:17] + at_rows[32:33]
    at_col = jnp.sum(jnp.where(diagonal, at_row, 0.0), axis=1, keepdims=True)
    drain_later = list(pending)
    arrive(got)
    for d in xd:
        pl.semaphore_signal(known, inc=1, device_id=xpeer(d), device_id_type=MESH)
    embedded = nn(of_token, d_r[...].reshape(T, E))
    cot = cot_v[...]
    dx, normed, dpre, gated, dng, dog = layer(
        embedded, cot, w, wout, ng[...], og[...], same
    )

    first_a = wacc_a.shape[4]
    first_b = wacc_b.shape[4]
    half = first_a + first_b
    shape_a, shape_b = wacc_a.shape[1:], wacc_b.shape[1:]
    wacc_a[0] = tn(normed, dpre[:, :first_a]).reshape(shape_a)
    wacc_a[1] = tn(normed, dpre[:, half:]).reshape(shape_a)
    w1s_a[...] = wacc_a[other].astype(BF16)
    chunks = far_first(n) + [0]
    hop_a = {d: start([remote(w1s_a.at[vat(d)], w1r_a.at[vat(d)], p1s.at[0, d], p1r.at[0, d], cpeer)]) for d in chunks}
    wacc_b[0] = tn(normed, dpre[:, first_a:half]).reshape(shape_b)
    wacc_b[1] = tn(gated, cot).reshape(shape_b)
    w1s_b[...] = wacc_b[other].astype(BF16)
    hop_b = {d: start([remote(w1s_b.at[uat(d)], w1r_b.at[uat(d)], p1s.at[1, d], p1r.at[1, d], cpeer)]) for d in chunks}
    ga_c[c] = jnp.concatenate([dng, dog, jnp.zeros((6, E), F32)], axis=0)
    got_ga = across(2, ga_c.at[c], ga_c.at[c])

    dx_high, dx_low = split2(dx)
    slot_grad = (nn(of_slot, dx_high) + nn(of_slot, dx_low)).astype(BF16)
    e_s[...] = slot_grad.reshape(shards, cap, E)
    g_r[shard] = e_s[shard]
    got_grad = to_plane(1, e_s, g_r)

    pl.semaphore_wait(known, nx - 1)
    for d in chunks:
        for k, hop, at, wacc, w1r, acc, w2s, w2r in (
            (0, hop_a, uat(d), wacc_a, w1r_a, acc_a, w2s_a, w2r_a),
            (1, hop_b, vat(d), wacc_b, w1r_b, acc_b, w2s_b, w2r_b),
        ):
            arrive(hop[d])
            summed = wacc[c, at] + w1r[at].astype(F32)
            acc[at] = summed
            w2s[at] = summed.astype(BF16)
            hop[d] = start([
                remote(w2s.at[at, xat(e)], w2r.at[at, e - 1], p2s.at[k, d, e], p2r.at[k, d, e], xpeer(e))
                for e in xd
            ])
    arrive(got_ga)
    ga_x[x] = ga_c[0] + ga_c[1]
    got_ga = along_x(0, lambda d: ga_x.at[x], lambda d: ga_x.at[x])
    for copy in drain_later:
        copy.wait_send()
    del pending[: len(drain_later)]
    got = [[], []]
    own = [None, None]
    for d in chunks:
        for k, hop, at, acc, w2r, w3s, w3r, peer in (
            (0, hop_a, uat(d), acc_a, w2r_a, w3s_a, w3r_a, ushard(d)),
            (1, hop_b, vat(d), acc_b, w2r_b, w3s_b, w3r_b, vshard(d)),
        ):
            arrive(hop[d])
            total = acc[at, x]
            for e in range(nx - 1):
                total = total + w2r[at, e].astype(F32)
            if d:
                w3s[d - 1] = total.astype(BF16)
                got[k] += start([
                    remote(w3s.at[d - 1], w3r.at[d - 1], p3s.at[k, d], p3r.at[k, d], {"shard": peer})
                ])
            else:
                own[k] = total
    arrive(got_ga)
    gsum = ga_x[0]
    for k in range(1, nx):
        gsum = gsum + ga_x[k]
    ga_z[z] = gsum
    got_ga = along_z(1, lambda d: ga_z.at[z], lambda d: ga_z.at[z])

    arrive(got_grad)
    sums = nn(pairs, g_r[...].reshape(T, E))
    square = lane_mean(sums * sums)
    scale = (-LEARN_RATE) * first * lax.rsqrt(at_col + square + EPSILON)
    dall[rep] = (sums * scale).astype(BF16)
    square_row = jnp.sum(jnp.where(diagonal, square * first, 0.0), axis=0, keepdims=True)
    mall[rep] = jnp.concatenate([asked_row, square_row, jnp.zeros((6, T), F32)], axis=0)
    got_d = along_x(1, lambda d: dall.at[rep], lambda d: dall.at[rep])
    got_m = along_x(2, lambda d: mall.at[rep], lambda d: mall.at[rep])
    forwards = across(3, dall.at[rep], dall.at[rep]) + across(4, mall.at[rep], mall.at[rep])

    hop = [None, None]
    for k, w3r, w4, at, other_at in ((0, w3r_a, w4_a, vpos, vshard), (1, w3r_b, w4_b, upos, ushard)):
        arrive(got[k])
        total = own[k]
        for d in range(1, n):
            total = total + w3r[d - 1].astype(F32)
        w4[at] = total.astype(BF16)
        hop[k] = start([
            remote(w4.at[at], w4.at[at], p4s.at[k, d], p4r.at[k, d], {"shard": other_at(d)}) for d in far_first(n)
        ])
    arrive(got_ga)
    gsum = ga_z[0]
    for k in range(1, nz):
        gsum = gsum + ga_z[k]
    ga_y[y] = gsum
    got_ga = along_y(2, lambda d: ga_y.at[y], lambda d: ga_y.at[y])

    arrive(got_d)
    arrive(got_m)
    for d in range(1, nx):
        source = xat(nx - d) * 2 + c
        forwards += across(3 + 2 * d, dall.at[source], dall.at[source])
        forwards += across(4 + 2 * d, mall.at[source], mall.at[source])

    scale = 1.0 / math.sqrt(T * shards * reps)
    got = [None, None]
    mine = [None, None]
    for k, w4, fin, at, peer, s1, s2 in (
        (0, w4_a, fin_a, ux_at(0, 0), ux, as_, ar), (1, w4_b, fin_b, vx_at(0, 0), vx, bs, br)
    ):
        arrive(hop[k])
        total = w4[0].astype(F32)
        for j in range(1, n):
            total = total + w4[j].astype(F32)
        fin[c, at] = (total * scale).astype(BF16)
        mine[k] = fin.at[c, at]
        got[k] = start([
            remote(mine[k], mine[k], s1.at[a * nx + b], s2.at[a * nx + b], peer(a, b)) for a, b in box
        ])
    from_c = start([
        remote(mine[0], mine[0], gas.at[0], gar.at[0], cpeer),
        remote(mine[1], mine[1], gbs.at[0], gbr.at[0], cpeer),
    ])

    arrive(forwards)
    squares = jnp.concatenate([mall[k][1:2, :] for k in range(reps)], axis=1)
    sq_high, sq_low = split2(squares)
    both = jnp.concatenate([jnp.broadcast_to(t, (16, reps * T)) for t in (sq_high, sq_low)], axis=0)
    asked = jnp.concatenate([mall[k][0:1, :] for k in range(reps)], axis=1)
    changes = dall[...].reshape(reps * T, E)
    share = 1.0 / reps
    for block in range(rows_dev // T):
        row_id = (iota((T, 1), 0) + block * T).astype(F32)
        hot = (row_id == asked).astype(F32).astype(BF16)
        rows_out[block * T : (block + 1) * T, :] = nn(hot, changes) * share
        add = nt(both, hot)
        state_out[block : block + 1, :] = state[block : block + 1, :] + (add[0:1] + add[16:17]) * share

    arrive(got_ga)
    gsum = ga_y[0]
    for k in range(1, ny):
        gsum = gsum + ga_y[k]
    gains_out[...] = gsum * scale
    late = 2 * len(box) + 2
    for copy in pending[:-late]:
        copy.wait_send()
    del pending[:-late]
    parts = [
        (hops(a, n) + hops(b, nx), k, a, b, copy) for k in range(2) for (a, b), copy in zip(box, got[k])
    ]
    parts.sort(key=lambda p: p[:4])
    for _, which, a, b, copy in parts:
        arrive([copy])
        e = a * nx + b
        if which == 0:
            part = fin_a.at[c, ux_at(n - a, nx - b)]
            from_c += start([remote(part, part, gas.at[e], gar.at[e], cpeer)])
        else:
            part = fin_b.at[c, vx_at(n - a, nx - b)]
            from_c += start([remote(part, part, gbs.at[e], gbr.at[e], cpeer)])
    arrive(from_c)
    fina_out[...] = fin_a[...]
    finb_out[...] = fin_b[...]
    drain()


def write_kernel(rows, state, fin_a, fin_b, gains, rows_o, state_o, uvqk_o, wout_o, gains_o, uvqk, wout, sem):
    first = pltpu.make_async_copy(rows, rows_o, sem.at[0])
    first.start()
    at = fin_a.shape[2]
    half = at + fin_b.shape[2]
    uvqk[:, :at] = fin_a[0].astype(F32)
    uvqk[:, at:half] = fin_b[0].astype(F32)
    uvqk[:, half:] = fin_a[1].astype(F32)
    second = pltpu.make_async_copy(uvqk, uvqk_o, sem.at[1])
    second.start()
    wout[...] = fin_b[1].astype(F32)
    third = pltpu.make_async_copy(wout, wout_o, sem.at[2])
    third.start()
    state_o[...] = state[...]
    gains_o[...] = gains[0:2, :]
    first.wait()
    second.wait()
    third.wait()


def on_device(nz, ny, nx, request_rows, token_slot, seq_lengths, cotangent, table_slab,
              adagrad_state, w_uvqk, w_out, norm_gain, out_gain):
    rows_dev = table_slab.shape[0]
    shards, reps = nz * ny, 2 * nx
    cap = T // shards
    ca, cb = nz * nx, ny * nx
    chunk_a, chunk_b = (E // ca, 384), (E // cb, 256)
    vmem = pl.BlockSpec(memory_space=pltpu.VMEM)
    hbm = pl.BlockSpec(memory_space=pltpu.HBM)
    dma = pltpu.SemaphoreType.DMA
    V = pltpu.VMEM
    I32 = jnp.int32
    rows, state, fin_a, fin_b, gains = pl.pallas_call(
        functools.partial(step_kernel, nz, ny, nx),
        out_shape=(
            jax.ShapeDtypeStruct((rows_dev, E), F32),
            jax.ShapeDtypeStruct((rows_dev // T, T), F32),
            jax.ShapeDtypeStruct((2, ca, *chunk_a), BF16),
            jax.ShapeDtypeStruct((2, cb, *chunk_b), BF16),
            jax.ShapeDtypeStruct((8, E), F32),
        ),
        in_specs=[hbm] * 10,
        out_specs=(vmem,) * 5,
        scratch_shapes=[
            pltpu.SMEM((1, SEQS), I32), V((1, 1, T), I32), V((1, T), I32), V((T, E), BF16),
            V((rows_dev, E), F32), V((rows_dev // T, T), F32), V((E, 4 * E), BF16), V((E, E), BF16),
            V((1, E), F32), V((1, E), F32),
            V((nz, 1, T), I32), V((ny, 1, T), I32),
            V((shards, cap, E), BF16), V((shards, cap, E), BF16),
            V((shards, cap, E), BF16), V((shards, cap, E), BF16),
            V((T, rows_dev), BF16), V((rows_dev, E), BF16),
            V((reps, T, E), BF16), V((reps, 8, T), F32),
            V((2, nz, nx, *chunk_a), F32), V((2, nz, nx, *chunk_b), F32),
            V((nz, nx, *chunk_a), BF16), V((nz, nx, *chunk_b), BF16),
            V((nz, nx, *chunk_a), BF16), V((nz, nx, *chunk_b), BF16),
            V((nz, nx, *chunk_a), F32), V((nz, nx, *chunk_b), F32),
            V((nz, nx, *chunk_a), BF16), V((nz, nx, *chunk_b), BF16),
            V((nz, nx - 1, *chunk_a), BF16), V((nz, nx - 1, *chunk_b), BF16),
            V((nz - 1, *chunk_a), BF16), V((nz - 1, *chunk_b), BF16),
            V((nz - 1, *chunk_a), BF16), V((nz - 1, *chunk_b), BF16),
            V((nz, *chunk_a), BF16), V((nz, *chunk_b), BF16),
            V((2, ca, *chunk_a), BF16), V((2, cb, *chunk_b), BF16),
            V((2, 8, E), F32), V((nx, 8, E), F32), V((nz, 8, E), F32), V((ny, 8, E), F32),
            dma((10,)),
            dma((3, nz)), dma((3, nz)), dma((3, ny)), dma((3, ny)),
            dma((3, nx)), dma((3, nx)), dma((3 + 2 * nx,)), dma((3 + 2 * nx,)),
            dma((2, shards)), dma((2, shards)),
            dma((2, nz)), dma((2, nz)), dma((2, nz, nx)), dma((2, nz, nx)),
            dma((2, nz)), dma((2, nz)), dma((2, nz)), dma((2, nz)),
            dma((ca,)), dma((ca,)), dma((cb,)), dma((cb,)),
            dma((ca,)), dma((ca,)), dma((cb,)), dma((cb,)),
            pltpu.SemaphoreType.REGULAR,
        ],
        compiler_params=pltpu.CompilerParams(
            collective_id=0, has_side_effects=True, vmem_limit_bytes=24 << 20
        ),
        name="step",
    )(
        *(
            pltpu.with_memory_space_constraint(a, pltpu.HBM)
            for a in (
                seq_lengths.reshape(1, SEQS),
                request_rows.reshape(1, 1, T),
                token_slot,
                cotangent[0],
                table_slab,
                adagrad_state.reshape(rows_dev // T, T),
                w_uvqk,
                w_out,
                norm_gain.reshape(1, E),
                out_gain.reshape(1, E),
            )
        )
    )
    rows, state, uvqk, wout, gains = pl.pallas_call(
        write_kernel,
        out_shape=(
            jax.ShapeDtypeStruct((rows_dev, E), F32),
            jax.ShapeDtypeStruct((rows_dev // T, T), F32),
            jax.ShapeDtypeStruct((E, 4 * E), F32),
            jax.ShapeDtypeStruct((E, E), F32),
            jax.ShapeDtypeStruct((2, E), F32),
        ),
        in_specs=[vmem] * 5,
        out_specs=(hbm, vmem, hbm, hbm, vmem),
        scratch_shapes=[V((E, 4 * E), F32), V((E, E), F32), dma((3,))],
        compiler_params=pltpu.CompilerParams(vmem_limit_bytes=24 << 20),
        name="write",
    )(rows, state, fin_a.reshape(2, E, 384), fin_b.reshape(2, E, 256), gains)
    return rows, state.reshape(rows_dev), uvqk, wout, gains


def solution(mesh):
    shards, reps = mesh.shape["shard"], mesh.shape["replica"]
    side = math.isqrt(shards)
    return jax.shard_map(
        functools.partial(on_device, side, shards // side, reps // 2),
        mesh=mesh,
        in_specs=(
            P("replica", "shard", None),
            P("replica", "shard"),
            P("replica", "shard", None),
            P("replica", "shard", None),
            P("shard", None),
            P("shard"),
            P(),
            P(),
            P(),
            P(),
        ),
        out_specs=(P("shard", None), P("shard"), P(), P(), P()),
        check_vma=False,
    )
```

```python
import functools
import math

import jax
import jax.numpy as jnp
from jax import lax
from jax.experimental import pallas as pl
from jax.experimental.pallas import tpu as pltpu
from jax.sharding import PartitionSpec as P

HEADS = 4
MAXLEN = 48
SEQS = 8
EPSILON = 1e-08
LEARN_RATE = 0.5
E = 256
T = 128
F32 = jnp.float32
BF16 = jnp.bfloat16
MESH = pl.DeviceIdType.MESH


def far_first(n):
    return sorted(range(1, n), key=lambda d: -min(d, n - d))


def nn(a, b):
    return lax.dot_general(a, b, (((1,), (0,)), ((), ())), preferred_element_type=F32)


def nt(a, b):
    return lax.dot_general(a, b, (((1,), (1,)), ((), ())), preferred_element_type=F32)


def tn(a, b):
    return lax.dot_general(a, b, (((0,), (0,)), ((), ())), preferred_element_type=F32)


def iota(shape, dim):
    return lax.broadcasted_iota(jnp.int32, shape, dim)


def lane_mean(x):
    return jnp.sum(x, axis=1, keepdims=True) * (1.0 / x.shape[1])


def split2(x):
    high = x.astype(BF16)
    return high, (x - high.astype(F32)).astype(BF16)


def layer(x, cot, w_ref, wout_ref, ng, og, same, early):
    center = x - lane_mean(x)
    rstd = lax.rsqrt(lane_mean(center * center) + 1e-05)
    xhat = center * rstd
    normed = (xhat * ng).astype(BF16)
    pre = nn(normed, w_ref[...])
    sig = lax.logistic(pre)
    proj = pre * sig
    dsilu = sig * (1.0 + pre * (1.0 - sig))
    u = proj[:, :E]
    low = iota((T, 128), 1) < 64
    zero = jnp.zeros((T, 128), BF16)
    pairs, att = [], []
    for p in range(2):
        at = p * 128
        vp = proj[:, E + at : E + at + 128].astype(BF16)
        qp = proj[:, 2 * E + at : 2 * E + at + 128].astype(BF16)
        kp = proj[:, 3 * E + at : 3 * E + at + 128].astype(BF16)
        heads, total = [], None
        for h in range(2):
            mine = low if h == 0 else jnp.logical_not(low)
            qh, kh = jnp.where(mine, qp, zero), jnp.where(mine, kp, zero)
            s = nt(qh, kp) * 0.125
            sg = lax.logistic(s)
            weights = jnp.where(same, s * sg * (1.0 / MAXLEN), 0.0).astype(BF16)
            slope = jnp.where(same, sg * (1.0 + s * (1.0 - sg)) * (0.125 / MAXLEN), 0.0)
            part = nn(weights, jnp.where(mine, vp, zero))
            total = part if total is None else total + part
            heads.append((mine, qh, kh, weights, slope))
        pairs.append((vp, heads))
        att.append(total)
    attended = jnp.concatenate(att, axis=1)
    center2 = attended - lane_mean(attended)
    rstd2 = lax.rsqrt(lane_mean(center2 * center2) + 1e-05)
    ahat = center2 * rstd2
    gated = (ahat * og * u).astype(BF16)
    dgated = nt(cot, wout_ref[...]).astype(BF16).astype(F32)
    au = ahat * u
    dog = jnp.sum(dgated * au, axis=0, keepdims=True)
    dgo = dgated * og
    du = dgo * ahat
    dpre_u = (du * dsilu[:, :E]).astype(BF16)
    early(normed, dpre_u, gated)
    dahat = dgo * u
    datt = rstd2 * (dahat - lane_mean(dahat) - ahat * lane_mean(dahat * ahat))
    datt = datt.astype(BF16)
    dvs, dqs, dks = [], [], []
    for p in range(2):
        vp, heads = pairs[p]
        dp = datt[:, p * 128 : p * 128 + 128]
        dv = dq = dk = None
        for mine, qh, kh, weights, slope in heads:
            dh = jnp.where(mine, dp, zero)
            dw = nt(dh, vp).astype(BF16).astype(F32)
            ds = (dw * slope).astype(BF16)
            a, b, c = tn(weights, dh), nn(ds, kh), tn(ds, qh)
            dv, dq, dk = (a, b, c) if dv is None else (dv + a, dq + b, dk + c)
        dvs.append(dv)
        dqs.append(dq)
        dks.append(dk)
    rounded = [t.astype(BF16).astype(F32) for t in (*dvs, *dqs, *dks)]
    dpre = (jnp.concatenate(rounded, axis=1) * dsilu[:, E:]).astype(BF16)
    dnormed = nt(jnp.concatenate([dpre_u, dpre], axis=1), w_ref[...]).astype(BF16).astype(F32)
    dng = jnp.sum(dnormed * xhat, axis=0, keepdims=True)
    dxhat = dnormed * ng
    dx = rstd * (dxhat - lane_mean(dxhat) - xhat * lane_mean(dxhat * xhat)) + cot.astype(F32)
    return dx, normed, dpre, dng, dog


def step_kernel(
    nz, ny, nx,
    lens_in, ids_in, slots_in, cot_in, table_in, state_in, w_in, wout_in, ng_in, og_in,
    rows_out, state_out, fin_a, fin_b, gains_out,
    lens, ids, slots, cot_v, table, state_v, w, wout, ng, og,
    iz, iy, a_s, d_r, e_s, g_r, hot_rows, table_b, dall, mall,
    wacc_a, wacc_b, w1s_a, w1s_b, w1r_a, w1r_b, acc_a, acc_b, w2s_a, w2s_b, w2r_a, w2r_b,
    w3s_a, w3s_b, w3r_a, w3r_b, w4_a, w4_b,
    ga_c, ga_x, ga_z, ga_y,
    ls, zs, zr, ys, yr, xs, xr, cs, cr, rs_s, rs_r, p1s, p1r, p2s, p2r, p3s, p3r, p4s, p4r,
    as_, ar, bs, br, gas, gar, gbs, gbr, known,
):
    shards, reps = nz * ny, 2 * nx
    cap = T // shards
    zb = T // nz
    lcap, lzb = int(math.log2(cap)), int(math.log2(zb))
    rows_dev = table.shape[0]
    shard, rep = lax.axis_index("shard"), lax.axis_index("replica")
    z, y = shard // ny, lax.rem(shard, ny)
    x, c = rep // 2, lax.rem(rep, 2)
    other = 1 - c
    zat = lambda d: lax.rem(z + d, nz)
    yat = lambda d: lax.rem(y + d, ny)
    xat = lambda d: lax.rem(x + d, nx)
    zpeer = lambda d: {"shard": zat(d) * ny + y}
    ypeer = lambda d: {"shard": z * ny + yat(d)}
    xpeer = lambda d: {"replica": xat(d) * 2 + c}
    cpeer = {"replica": x * 2 + other}
    zd, yd, xd = far_first(nz), far_first(ny), far_first(nx)
    hops = lambda d, n: min(d, n - d)
    plane = [(a, b) for a in range(nz) for b in range(ny) if a or b]
    plane.sort(key=lambda d: -(hops(d[0], nz) + hops(d[1], ny)))
    n = nz
    box = [(a, b) for a in range(n) for b in range(nx) if a or b]
    box.sort(key=lambda d: -(hops(d[0], n) + hops(d[1], nx)))
    upos, vpos = z + c * (y - z), y + c * (z - y)
    uat = lambda d: lax.rem(upos + d, n)
    vat = lambda d: lax.rem(vpos + d, n)
    ushard = lambda d: zat((1 - c) * d) * ny + yat(c * d)
    vshard = lambda d: zat(c * d) * ny + yat((1 - c) * d)
    ux_at = lambda a, b: uat(a) * nx + xat(b)
    vx_at = lambda a, b: vat(a) * nx + xat(b)
    ux = lambda a, b: {"shard": ushard(a), "replica": xat(b) * 2 + c}
    vx = lambda a, b: {"shard": vshard(a), "replica": xat(b) * 2 + c}

    def remote(src, dst, ssem, rsem, peer):
        return pltpu.make_async_remote_copy(
            src_ref=src, dst_ref=dst, send_sem=ssem, recv_sem=rsem,
            device_id=peer, device_id_type=MESH,
        )

    pending = []

    def drain():
        for copy in pending:
            copy.wait_send()
        pending.clear()

    def start(copies):
        for copy in copies:
            copy.start()
        pending.extend(copies)
        return copies

    def arrive(copies):
        for copy in copies:
            copy.wait_recv()

    def along_z(k, src, dst):
        return start([remote(src(d), dst(d), zs.at[k, d], zr.at[k, d], zpeer(d)) for d in zd])

    def along_y(k, src, dst):
        return start([remote(src(d), dst(d), ys.at[k, d], yr.at[k, d], ypeer(d)) for d in yd])

    def along_x(k, src, dst):
        return start([remote(src(d), dst(d), xs.at[k, d], xr.at[k, d], xpeer(d)) for d in xd])

    def across(k, src, dst):
        return start([remote(src, dst, cs.at[k], cr.at[k], cpeer)])

    def to_plane(k, src, dst):
        copies = []
        for a, b in plane:
            target = zat(a) * ny + yat(b)
            e = a * ny + b
            copies.append(
                remote(src.at[target], dst.at[shard], rs_s.at[k, e], rs_r.at[k, e], {"shard": target})
            )
        return start(copies)

    barrier = pltpu.get_barrier_semaphore()
    peers = [zpeer(d) for d in zd] + [ypeer(d) for d in yd] + [xpeer(d) for d in xd] + [cpeer]
    for peer in peers:
        pl.semaphore_signal(barrier, inc=1, device_id=peer, device_id_type=MESH)
    sources = (ids_in, lens_in, slots_in, state_in, ng_in, og_in, table_in, cot_in, w_in, wout_in)
    targets = (ids, lens, slots, state_v, ng, og, table, cot_v, w, wout)
    loads = [
        pltpu.make_async_copy(src, dst, ls.at[k]) for k, (src, dst) in enumerate(zip(sources, targets))
    ]
    for load in loads:
        load.start()

    for load in loads[:6]:
        load.wait()
    iz[z] = ids[0]
    row_i, lane_i = iota((T, T), 0), iota((T, T), 1)
    diagonal = row_i == lane_i
    ends = jnp.int32(0)
    seg_row = jnp.zeros((8, T), jnp.int32)
    seg_col = jnp.zeros((T, T), jnp.int32)
    row_t = iota((8, T), 1)
    for k in range(SEQS):
        ends = ends + lens[0, k]
        seg_row = seg_row + (row_t >= ends).astype(jnp.int32)
        seg_col = seg_col + (row_i >= ends).astype(jnp.int32)
    same = (seg_col == seg_row[0:1, :]) & (row_i >= lane_i)
    slot = slots[...].astype(F32)
    slot_col = jnp.sum(jnp.where(diagonal, slot, 0.0), axis=1, keepdims=True)
    of_slot = (row_i.astype(F32) == slot).astype(F32).astype(BF16)
    of_token = (lane_i.astype(F32) == slot_col).astype(F32).astype(BF16)

    pl.semaphore_wait(barrier, len(peers))

    got = along_z(0, lambda d: ids.at[0], lambda d: iz.at[z])
    loads[6].wait()
    table_b[...] = table[...].astype(BF16)
    arrive(got)
    total = jnp.zeros((8, T), jnp.int32)
    for s in range(nz):
        row = jnp.broadcast_to(iz[s], (8, T))
        row = jnp.where((row_t >> lzb) == z, row, 0)
        total = total + pltpu.roll(row, lax.rem((s - z) * zb + T, T), 1)
    iy[y] = total[0:1, :]
    got = along_y(0, lambda d: iy.at[y], lambda d: iy.at[y])
    for load in loads[7:]:
        load.wait()
    arrive(got)
    total = jnp.zeros((8, T), jnp.int32)
    for s in range(ny):
        row = jnp.broadcast_to(iy[s], (8, T))
        row = jnp.where(((row_t >> lcap) & (ny - 1)) == y, row, 0)
        total = total + pltpu.roll(row, lax.rem((s - y) * cap + T, T), 1)
    asked_row = total[0:1, :].astype(F32)
    asked_col = jnp.sum(jnp.where(diagonal, asked_row, 0.0), axis=1, keepdims=True)
    table_row = iota((1, rows_dev), 1).astype(F32)
    hot_rows[...] = (table_row == asked_col).astype(F32).astype(BF16)

    found = nn(hot_rows[...], table_b[...]).astype(BF16)
    a_s[...] = found.reshape(shards, cap, E)
    d_r[shard] = a_s[shard]
    got = to_plane(0, a_s, d_r)
    hot = hot_rows[...]
    pairs = nt(hot, hot)
    earlier = jnp.sum(jnp.where(lane_i < row_i, pairs, 0.0), axis=1, keepdims=True)
    first = jnp.where(earlier < 0.5, 1.0, 0.0)
    pairs = pairs.astype(BF16)
    state = state_v[...]
    flat = jnp.concatenate([state[k : k + 1, :] for k in range(rows_dev // T)], axis=1)
    high = flat.astype(BF16)
    rest = flat - high.astype(F32)
    mid = rest.astype(BF16)
    low = (rest - mid.astype(F32)).astype(BF16)
    three = jnp.concatenate(
        [jnp.broadcast_to(t, (16, rows_dev)) for t in (high, mid, low)], axis=0
    )
    at_rows = nt(three, hot)
    at_row = at_rows[0:1] + at_rows[16:17] + at_rows[32:33]
    at_col = jnp.sum(jnp.where(diagonal, at_row, 0.0), axis=1, keepdims=True)
    drain_later = list(pending)
    arrive(got)
    for d in xd:
        pl.semaphore_signal(known, inc=1, device_id=xpeer(d), device_id_type=MESH)
    embedded = nn(of_token, d_r[...].reshape(T, E))
    cot = cot_v[...]
    chunks = far_first(n) + [0]
    hop_b = {}

    def early(normed, dpre_u, gated):
        wacc_b[0] = tn(normed, dpre_u).reshape(wacc_b.shape[1:])
        wacc_b[1] = tn(gated, cot).reshape(wacc_b.shape[1:])
        w1s_b[...] = wacc_b[other].astype(BF16)
        for d in chunks:
            hop_b[d] = start(
                [remote(w1s_b.at[uat(d)], w1r_b.at[uat(d)], p1s.at[1, d], p1r.at[1, d], cpeer)]
            )

    dx, normed, dpre, dng, dog = layer(
        embedded, cot, w, wout, ng[...], og[...], same, early
    )

    wide = wacc_a.shape[4]
    wacc_a[0] = tn(normed, dpre[:, :wide]).reshape(wacc_a.shape[1:])
    wacc_a[1] = tn(normed, dpre[:, wide:]).reshape(wacc_a.shape[1:])
    w1s_a[...] = wacc_a[other].astype(BF16)
    hop_a = {d: start([remote(w1s_a.at[vat(d)], w1r_a.at[vat(d)], p1s.at[0, d], p1r.at[0, d], cpeer)]) for d in chunks}
    pl.semaphore_wait(known, nx - 1)

    def over_x(k, hop, d, at, wacc, w1r, acc, w2s, w2r):
        arrive(hop[d])
        summed = wacc[c, at] + w1r[at].astype(F32)
        acc[at] = summed
        w2s[at] = summed.astype(BF16)
        hop[d] = start([
            remote(w2s.at[at, xat(e)], w2r.at[at, e - 1], p2s.at[k, d, e], p2r.at[k, d, e], xpeer(e))
            for e in xd
        ])

    for d in chunks:
        over_x(1, hop_b, d, vat(d), wacc_b, w1r_b, acc_b, w2s_b, w2r_b)
    ga_c[c] = jnp.concatenate([dng, dog, jnp.zeros((6, E), F32)], axis=0)
    got_ga = across(2, ga_c.at[c], ga_c.at[c])

    dx_high, dx_low = split2(dx)
    slot_grad = (nn(of_slot, dx_high) + nn(of_slot, dx_low)).astype(BF16)
    e_s[...] = slot_grad.reshape(shards, cap, E)
    g_r[shard] = e_s[shard]
    got_grad = to_plane(1, e_s, g_r)

    for d in chunks:
        over_x(0, hop_a, d, uat(d), wacc_a, w1r_a, acc_a, w2s_a, w2r_a)
    arrive(got_ga)
    ga_x[x] = ga_c[0] + ga_c[1]
    got_ga = along_x(0, lambda d: ga_x.at[x], lambda d: ga_x.at[x])
    for copy in drain_later:
        copy.wait_send()
    del pending[: len(drain_later)]
    got = [[], []]
    own = [None, None]
    for k, hop, at_of, acc, w2r, w3s, w3r, peer in (
        (1, hop_b, vat, acc_b, w2r_b, w3s_b, w3r_b, vshard),
        (0, hop_a, uat, acc_a, w2r_a, w3s_a, w3r_a, ushard),
    ):
        for d in chunks:
            at = at_of(d)
            arrive(hop[d])
            total = acc[at, x]
            for e in range(nx - 1):
                total = total + w2r[at, e].astype(F32)
            if d:
                w3s[d - 1] = total.astype(BF16)
                got[k] += start([
                    remote(w3s.at[d - 1], w3r.at[d - 1], p3s.at[k, d], p3r.at[k, d], {"shard": peer(d)})
                ])
            else:
                own[k] = total
    arrive(got_ga)
    gsum = ga_x[0]
    for k in range(1, nx):
        gsum = gsum + ga_x[k]
    ga_z[z] = gsum
    got_ga = along_z(1, lambda d: ga_z.at[z], lambda d: ga_z.at[z])

    arrive(got_grad)
    sums = nn(pairs, g_r[...].reshape(T, E))
    square = lane_mean(sums * sums)
    scale = (-LEARN_RATE) * first * lax.rsqrt(at_col + square + EPSILON)
    dall[rep] = (sums * scale).astype(BF16)
    square_row = jnp.sum(jnp.where(diagonal, square * first, 0.0), axis=0, keepdims=True)
    mall[rep] = jnp.concatenate([asked_row, square_row, jnp.zeros((6, T), F32)], axis=0)
    got_d = along_x(1, lambda d: dall.at[rep], lambda d: dall.at[rep])
    got_m = along_x(2, lambda d: mall.at[rep], lambda d: mall.at[rep])
    forwards = across(3, dall.at[rep], dall.at[rep]) + across(4, mall.at[rep], mall.at[rep])

    hop = [None, None]
    for k, w3r, w4, at, other_at in ((1, w3r_b, w4_b, upos, ushard), (0, w3r_a, w4_a, vpos, vshard)):
        arrive(got[k])
        total = own[k]
        for d in range(1, n):
            total = total + w3r[d - 1].astype(F32)
        w4[at] = total.astype(BF16)
        hop[k] = start([
            remote(w4.at[at], w4.at[at], p4s.at[k, d], p4r.at[k, d], {"shard": other_at(d)}) for d in far_first(n)
        ])
    arrive(got_ga)
    gsum = ga_z[0]
    for k in range(1, nz):
        gsum = gsum + ga_z[k]
    ga_y[y] = gsum
    got_ga = along_y(2, lambda d: ga_y.at[y], lambda d: ga_y.at[y])

    arrive(got_d)
    arrive(got_m)
    for d in range(1, nx):
        source = xat(nx - d) * 2 + c
        forwards += across(3 + 2 * d, dall.at[source], dall.at[source])
        forwards += across(4 + 2 * d, mall.at[source], mall.at[source])

    scale = 1.0 / math.sqrt(T * shards * reps)
    got = [None, None]
    mine = [None, None]
    for k, w4, fin, at, peer, s1, s2 in (
        (1, w4_b, fin_b, vx_at(0, 0), vx, bs, br), (0, w4_a, fin_a, ux_at(0, 0), ux, as_, ar)
    ):
        arrive(hop[k])
        total = w4[0].astype(F32)
        for j in range(1, n):
            total = total + w4[j].astype(F32)
        fin[c, at] = (total * scale).astype(BF16)
        mine[k] = fin.at[c, at]
        got[k] = start([
            remote(mine[k], mine[k], s1.at[a * nx + b], s2.at[a * nx + b], peer(a, b)) for a, b in box
        ])
    from_c = start([
        remote(mine[0], mine[0], gas.at[0], gar.at[0], cpeer),
        remote(mine[1], mine[1], gbs.at[0], gbr.at[0], cpeer),
    ])

    arrive(forwards)
    squares = jnp.concatenate([mall[k][1:2, :] for k in range(reps)], axis=1)
    sq_high, sq_low = split2(squares)
    both = jnp.concatenate([jnp.broadcast_to(t, (16, reps * T)) for t in (sq_high, sq_low)], axis=0)
    asked = jnp.concatenate([mall[k][0:1, :] for k in range(reps)], axis=1)
    changes = dall[...].reshape(reps * T, E)
    share = 1.0 / reps
    for block in range(rows_dev // T):
        row_id = (iota((T, 1), 0) + block * T).astype(F32)
        hot = (row_id == asked).astype(F32).astype(BF16)
        rows_out[block * T : (block + 1) * T, :] = nn(hot, changes) * share
        add = nt(both, hot)
        state_out[block : block + 1, :] = state[block : block + 1, :] + (add[0:1] + add[16:17]) * share

    arrive(got_ga)
    gsum = ga_y[0]
    for k in range(1, ny):
        gsum = gsum + ga_y[k]
    gains_out[...] = gsum * scale
    late = 2 * len(box) + 2
    for copy in pending[:-late]:
        copy.wait_send()
    del pending[:-late]
    parts = [
        (hops(a, n) + hops(b, nx), k, a, b, copy) for k in range(2) for (a, b), copy in zip(box, got[k])
    ]
    parts.sort(key=lambda p: p[:4])
    for _, which, a, b, copy in parts:
        arrive([copy])
        copy.wait_send()
        pending[:] = [p for p in pending if p is not copy]
        e = a * nx + b
        if which == 0:
            part = fin_a.at[c, ux_at(n - a, nx - b)]
            from_c += start([remote(part, part, gas.at[e], gar.at[e], cpeer)])
        else:
            part = fin_b.at[c, vx_at(n - a, nx - b)]
            from_c += start([remote(part, part, gbs.at[e], gbr.at[e], cpeer)])
    arrive(from_c)
    drain()


def write_kernel(rows, state, fin_a, fin_b, gains, rows_o, state_o, uvqk_o, wout_o, gains_o, uvqk, wout, sem):
    first = pltpu.make_async_copy(rows, rows_o, sem.at[0])
    first.start()
    at = fin_a.shape[2]
    half = at + fin_b.shape[2]
    uvqk[:, : half - at] = fin_b[0].astype(F32)
    uvqk[:, half - at : half] = fin_a[0].astype(F32)
    uvqk[:, half:] = fin_a[1].astype(F32)
    second = pltpu.make_async_copy(uvqk, uvqk_o, sem.at[1])
    second.start()
    wout[...] = fin_b[1].astype(F32)
    third = pltpu.make_async_copy(wout, wout_o, sem.at[2])
    third.start()
    state_o[...] = state[...]
    gains_o[...] = gains[0:2, :]
    first.wait()
    second.wait()
    third.wait()


def on_device(nz, ny, nx, request_rows, token_slot, seq_lengths, cotangent, table_slab,
              adagrad_state, w_uvqk, w_out, norm_gain, out_gain):
    rows_dev = table_slab.shape[0]
    shards, reps = nz * ny, 2 * nx
    cap = T // shards
    ca, cb = nz * nx, ny * nx
    chunk_a, chunk_b = (E // ca, 384), (E // cb, 256)
    vmem = pl.BlockSpec(memory_space=pltpu.VMEM)
    hbm = pl.BlockSpec(memory_space=pltpu.HBM)
    dma = pltpu.SemaphoreType.DMA
    V = pltpu.VMEM
    I32 = jnp.int32
    rows, state, fin_a, fin_b, gains = pl.pallas_call(
        functools.partial(step_kernel, nz, ny, nx),
        out_shape=(
            jax.ShapeDtypeStruct((rows_dev, E), F32),
            jax.ShapeDtypeStruct((rows_dev // T, T), F32),
            jax.ShapeDtypeStruct((2, ca, *chunk_a), BF16),
            jax.ShapeDtypeStruct((2, cb, *chunk_b), BF16),
            jax.ShapeDtypeStruct((8, E), F32),
        ),
        in_specs=[hbm] * 10,
        out_specs=(vmem,) * 5,
        scratch_shapes=[
            pltpu.SMEM((1, SEQS), I32), V((1, 1, T), I32), V((1, T), I32), V((T, E), BF16),
            V((rows_dev, E), F32), V((rows_dev // T, T), F32), V((E, 4 * E), BF16), V((E, E), BF16),
            V((1, E), F32), V((1, E), F32),
            V((nz, 1, T), I32), V((ny, 1, T), I32),
            V((shards, cap, E), BF16), V((shards, cap, E), BF16),
            V((shards, cap, E), BF16), V((shards, cap, E), BF16),
            V((T, rows_dev), BF16), V((rows_dev, E), BF16),
            V((reps, T, E), BF16), V((reps, 8, T), F32),
            V((2, nz, nx, *chunk_a), F32), V((2, nz, nx, *chunk_b), F32),
            V((nz, nx, *chunk_a), BF16), V((nz, nx, *chunk_b), BF16),
            V((nz, nx, *chunk_a), BF16), V((nz, nx, *chunk_b), BF16),
            V((nz, nx, *chunk_a), F32), V((nz, nx, *chunk_b), F32),
            V((nz, nx, *chunk_a), BF16), V((nz, nx, *chunk_b), BF16),
            V((nz, nx - 1, *chunk_a), BF16), V((nz, nx - 1, *chunk_b), BF16),
            V((nz - 1, *chunk_a), BF16), V((nz - 1, *chunk_b), BF16),
            V((nz - 1, *chunk_a), BF16), V((nz - 1, *chunk_b), BF16),
            V((nz, *chunk_a), BF16), V((nz, *chunk_b), BF16),
            V((2, 8, E), F32), V((nx, 8, E), F32), V((nz, 8, E), F32), V((ny, 8, E), F32),
            dma((10,)),
            dma((3, nz)), dma((3, nz)), dma((3, ny)), dma((3, ny)),
            dma((3, nx)), dma((3, nx)), dma((3 + 2 * nx,)), dma((3 + 2 * nx,)),
            dma((2, shards)), dma((2, shards)),
            dma((2, nz)), dma((2, nz)), dma((2, nz, nx)), dma((2, nz, nx)),
            dma((2, nz)), dma((2, nz)), dma((2, nz)), dma((2, nz)),
            dma((ca,)), dma((ca,)), dma((cb,)), dma((cb,)),
            dma((ca,)), dma((ca,)), dma((cb,)), dma((cb,)),
            pltpu.SemaphoreType.REGULAR,
        ],
        compiler_params=pltpu.CompilerParams(
            collective_id=0, has_side_effects=True, vmem_limit_bytes=24 << 20
        ),
        name="step",
    )(
        *(
            pltpu.with_memory_space_constraint(a, pltpu.HBM)
            for a in (
                seq_lengths.reshape(1, SEQS),
                request_rows.reshape(1, 1, T),
                token_slot,
                cotangent[0],
                table_slab,
                adagrad_state.reshape(rows_dev // T, T),
                w_uvqk,
                w_out,
                norm_gain.reshape(1, E),
                out_gain.reshape(1, E),
            )
        )
    )
    rows, state, uvqk, wout, gains = pl.pallas_call(
        write_kernel,
        out_shape=(
            jax.ShapeDtypeStruct((rows_dev, E), F32),
            jax.ShapeDtypeStruct((rows_dev // T, T), F32),
            jax.ShapeDtypeStruct((E, 4 * E), F32),
            jax.ShapeDtypeStruct((E, E), F32),
            jax.ShapeDtypeStruct((2, E), F32),
        ),
        in_specs=[vmem] * 5,
        out_specs=(hbm, vmem, hbm, hbm, vmem),
        scratch_shapes=[V((E, 4 * E), F32), V((E, E), F32), dma((3,))],
        compiler_params=pltpu.CompilerParams(vmem_limit_bytes=24 << 20),
        name="write",
    )(rows, state, fin_a.reshape(2, E, 384), fin_b.reshape(2, E, 256), gains)
    return rows, state.reshape(rows_dev), uvqk, wout, gains


def solution(mesh):
    shards, reps = mesh.shape["shard"], mesh.shape["replica"]
    side = math.isqrt(shards)
    return jax.shard_map(
        functools.partial(on_device, side, shards // side, reps // 2),
        mesh=mesh,
        in_specs=(
            P("replica", "shard", None),
            P("replica", "shard"),
            P("replica", "shard", None),
            P("replica", "shard", None),
            P("shard", None),
            P("shard"),
            P(),
            P(),
            P(),
            P(),
        ),
        out_specs=(P("shard", None), P("shard"), P(), P(), P()),
        check_vma=False,
    )
```

```python
import functools
import math

import jax
import jax.numpy as jnp
from jax import lax
from jax.experimental import pallas as pl
from jax.experimental.pallas import tpu as pltpu
from jax.sharding import PartitionSpec as P

HEADS = 4
MAXLEN = 48
SEQS = 8
EPSILON = 1e-08
LEARN_RATE = 0.5
E = 256
T = 128
F32 = jnp.float32
BF16 = jnp.bfloat16
MESH = pl.DeviceIdType.MESH


def far_first(n):
    return sorted(range(1, n), key=lambda d: -min(d, n - d))


def nn(a, b):
    return lax.dot_general(a, b, (((1,), (0,)), ((), ())), preferred_element_type=F32)


def nt(a, b):
    return lax.dot_general(a, b, (((1,), (1,)), ((), ())), preferred_element_type=F32)


def tn(a, b):
    return lax.dot_general(a, b, (((0,), (0,)), ((), ())), preferred_element_type=F32)


def iota(shape, dim):
    return lax.broadcasted_iota(jnp.int32, shape, dim)


def lane_mean(x):
    return jnp.sum(x, axis=1, keepdims=True) * (1.0 / x.shape[1])


def split2(x):
    high = x.astype(BF16)
    return high, (x - high.astype(F32)).astype(BF16)


def layer(x, cot, w_ref, wout_ref, ng, og, same, early):
    center = x - lane_mean(x)
    rstd = lax.rsqrt(lane_mean(center * center) + 1e-05)
    xhat = center * rstd
    normed = (xhat * ng).astype(BF16)
    pre = nn(normed, w_ref[...])
    sig = lax.logistic(pre)
    proj = pre * sig
    dsilu = sig * (1.0 + pre * (1.0 - sig))
    u = proj[:, :E]
    low = iota((T, 128), 1) < 64
    zero = jnp.zeros((T, 128), BF16)
    pairs, att = [], []
    for p in range(2):
        at = p * 128
        vp = proj[:, E + at : E + at + 128].astype(BF16)
        qp = proj[:, 2 * E + at : 2 * E + at + 128].astype(BF16)
        kp = proj[:, 3 * E + at : 3 * E + at + 128].astype(BF16)
        heads, total = [], None
        for h in range(2):
            mine = low if h == 0 else jnp.logical_not(low)
            qh, kh = jnp.where(mine, qp, zero), jnp.where(mine, kp, zero)
            s = nt(qh, kp) * 0.125
            sg = lax.logistic(s)
            weights = jnp.where(same, s * sg * (1.0 / MAXLEN), 0.0).astype(BF16)
            slope = jnp.where(same, sg * (1.0 + s * (1.0 - sg)) * (0.125 / MAXLEN), 0.0)
            part = nn(weights, jnp.where(mine, vp, zero))
            total = part if total is None else total + part
            heads.append((mine, qh, kh, weights, slope))
        pairs.append((vp, heads))
        att.append(total)
    attended = jnp.concatenate(att, axis=1)
    center2 = attended - lane_mean(attended)
    rstd2 = lax.rsqrt(lane_mean(center2 * center2) + 1e-05)
    ahat = center2 * rstd2
    gated = (ahat * og * u).astype(BF16)
    dgated = nt(cot, wout_ref[...]).astype(BF16).astype(F32)
    au = ahat * u
    dog = jnp.sum(dgated * au, axis=0, keepdims=True)
    dgo = dgated * og
    du = dgo * ahat
    dpre_u = (du * dsilu[:, :E]).astype(BF16)
    early(normed, dpre_u, gated)
    dahat = dgo * u
    datt = rstd2 * (dahat - lane_mean(dahat) - ahat * lane_mean(dahat * ahat))
    datt = datt.astype(BF16)
    dvs, dqs, dks = [], [], []
    for p in range(2):
        vp, heads = pairs[p]
        dp = datt[:, p * 128 : p * 128 + 128]
        dv = dq = dk = None
        for mine, qh, kh, weights, slope in heads:
            dh = jnp.where(mine, dp, zero)
            dw = nt(dh, vp).astype(BF16).astype(F32)
            ds = (dw * slope).astype(BF16)
            a, b, c = tn(weights, dh), nn(ds, kh), tn(ds, qh)
            dv, dq, dk = (a, b, c) if dv is None else (dv + a, dq + b, dk + c)
        dvs.append(dv)
        dqs.append(dq)
        dks.append(dk)
    rounded = [t.astype(BF16).astype(F32) for t in (*dvs, *dqs, *dks)]
    dpre = (jnp.concatenate(rounded, axis=1) * dsilu[:, E:]).astype(BF16)
    dnormed = nt(jnp.concatenate([dpre_u, dpre], axis=1), w_ref[...]).astype(BF16).astype(F32)
    dng = jnp.sum(dnormed * xhat, axis=0, keepdims=True)
    dxhat = dnormed * ng
    dx = rstd * (dxhat - lane_mean(dxhat) - xhat * lane_mean(dxhat * xhat)) + cot.astype(F32)
    return dx, normed, dpre, dng, dog


def step_kernel(
    nz, ny, nx,
    lens_in, ids_in, slots_in, cot_in, table_in, state_in, w_in, wout_in, ng_in, og_in,
    rows_out, state_out, fin_a, fin_b, gains_out,
    lens, ids, slots, cot_v, table, state_v, w, wout, ng, og,
    iz, iy, a_s, d_r, e_s, g_r, hot_rows, table_b, dall, mall,
    wacc_a, wacc_b, w1s_a, w1s_b, w1r_a, w1r_b, acc_a, acc_b, w2s_a, w2s_b, w2r_a, w2r_b,
    w3s_a, w3s_b, w3r_a, w3r_b, w4_a, w4_b,
    ga_c, ga_x, ga_z, ga_y,
    ls, zs, zr, ys, yr, xs, xr, cs, cr, rs_s, rs_r, p1s, p1r, p2s, p2r, p3s, p3r, p4s, p4r,
    as_, ar, bs, br, gas, gar, gbs, gbr, known,
):
    shards, reps = nz * ny, 2 * nx
    cap = T // shards
    zb = T // nz
    lcap, lzb = int(math.log2(cap)), int(math.log2(zb))
    rows_dev = table.shape[0]
    shard, rep = lax.axis_index("shard"), lax.axis_index("replica")
    z, y = shard // ny, lax.rem(shard, ny)
    x, c = rep // 2, lax.rem(rep, 2)
    other = 1 - c
    zat = lambda d: lax.rem(z + d, nz)
    yat = lambda d: lax.rem(y + d, ny)
    xat = lambda d: lax.rem(x + d, nx)
    zpeer = lambda d: {"shard": zat(d) * ny + y}
    ypeer = lambda d: {"shard": z * ny + yat(d)}
    xpeer = lambda d: {"replica": xat(d) * 2 + c}
    cpeer = {"replica": x * 2 + other}
    zd, yd, xd = far_first(nz), far_first(ny), far_first(nx)
    hops = lambda d, n: min(d, n - d)
    plane = [(a, b) for a in range(nz) for b in range(ny) if a or b]
    plane.sort(key=lambda d: -(hops(d[0], nz) + hops(d[1], ny)))
    n = nz
    box = [(a, b) for a in range(n) for b in range(nx) if a or b]
    box.sort(key=lambda d: -(hops(d[0], n) + hops(d[1], nx)))
    upos, vpos = z + c * (y - z), y + c * (z - y)
    uat = lambda d: lax.rem(upos + d, n)
    vat = lambda d: lax.rem(vpos + d, n)
    ushard = lambda d: zat((1 - c) * d) * ny + yat(c * d)
    vshard = lambda d: zat(c * d) * ny + yat((1 - c) * d)
    ux_at = lambda a, b: uat(a) * nx + xat(b)
    vx_at = lambda a, b: vat(a) * nx + xat(b)
    ux = lambda a, b: {"shard": ushard(a), "replica": xat(b) * 2 + c}
    vx = lambda a, b: {"shard": vshard(a), "replica": xat(b) * 2 + c}

    def remote(src, dst, ssem, rsem, peer):
        return pltpu.make_async_remote_copy(
            src_ref=src, dst_ref=dst, send_sem=ssem, recv_sem=rsem,
            device_id=peer, device_id_type=MESH,
        )

    pending = []

    def drain():
        for copy in pending:
            copy.wait_send()
        pending.clear()

    def start(copies):
        for copy in copies:
            copy.start()
        pending.extend(copies)
        return copies

    def arrive(copies):
        for copy in copies:
            copy.wait_recv()

    def along_z(k, src, dst):
        return start([remote(src(d), dst(d), zs.at[k, d], zr.at[k, d], zpeer(d)) for d in zd])

    def along_y(k, src, dst):
        return start([remote(src(d), dst(d), ys.at[k, d], yr.at[k, d], ypeer(d)) for d in yd])

    def along_x(k, src, dst):
        return start([remote(src(d), dst(d), xs.at[k, d], xr.at[k, d], xpeer(d)) for d in xd])

    def across(k, src, dst):
        return start([remote(src, dst, cs.at[k], cr.at[k], cpeer)])

    def to_plane(k, src, dst):
        copies = []
        for a, b in plane:
            target = zat(a) * ny + yat(b)
            e = a * ny + b
            copies.append(
                remote(src.at[target], dst.at[shard], rs_s.at[k, e], rs_r.at[k, e], {"shard": target})
            )
        return start(copies)

    barrier = pltpu.get_barrier_semaphore()
    peers = [zpeer(d) for d in zd] + [ypeer(d) for d in yd] + [xpeer(d) for d in xd] + [cpeer]
    for peer in peers:
        pl.semaphore_signal(barrier, inc=1, device_id=peer, device_id_type=MESH)
    sources = (ids_in, lens_in, slots_in, state_in, ng_in, og_in, table_in, cot_in, w_in, wout_in)
    targets = (ids, lens, slots, state_v, ng, og, table, cot_v, w, wout)
    loads = [
        pltpu.make_async_copy(src, dst, ls.at[k]) for k, (src, dst) in enumerate(zip(sources, targets))
    ]
    for load in loads:
        load.start()

    for load in loads[:6]:
        load.wait()
    iz[z] = ids[0]
    row_i, lane_i = iota((T, T), 0), iota((T, T), 1)
    diagonal = row_i == lane_i
    ends = jnp.int32(0)
    seg_row = jnp.zeros((8, T), jnp.int32)
    seg_col = jnp.zeros((T, T), jnp.int32)
    row_t = iota((8, T), 1)
    for k in range(SEQS):
        ends = ends + lens[0, k]
        seg_row = seg_row + (row_t >= ends).astype(jnp.int32)
        seg_col = seg_col + (row_i >= ends).astype(jnp.int32)
    same = (seg_col == seg_row[0:1, :]) & (row_i >= lane_i)
    slot = slots[...].astype(F32)
    slot_col = jnp.sum(jnp.where(diagonal, slot, 0.0), axis=1, keepdims=True)
    of_slot = (row_i.astype(F32) == slot).astype(F32).astype(BF16)
    of_token = (lane_i.astype(F32) == slot_col).astype(F32).astype(BF16)

    pl.semaphore_wait(barrier, len(peers))

    got = along_z(0, lambda d: ids.at[0], lambda d: iz.at[z])
    loads[6].wait()
    table_b[...] = table[...].astype(BF16)
    arrive(got)
    total = jnp.zeros((8, T), jnp.int32)
    for s in range(nz):
        row = jnp.broadcast_to(iz[s], (8, T))
        row = jnp.where((row_t >> lzb) == z, row, 0)
        total = total + pltpu.roll(row, lax.rem((s - z) * zb + T, T), 1)
    iy[y] = total[0:1, :]
    got = along_y(0, lambda d: iy.at[y], lambda d: iy.at[y])
    for load in loads[7:]:
        load.wait()
    arrive(got)
    total = jnp.zeros((8, T), jnp.int32)
    for s in range(ny):
        row = jnp.broadcast_to(iy[s], (8, T))
        row = jnp.where(((row_t >> lcap) & (ny - 1)) == y, row, 0)
        total = total + pltpu.roll(row, lax.rem((s - y) * cap + T, T), 1)
    asked_row = total[0:1, :].astype(F32)
    asked_col = jnp.sum(jnp.where(diagonal, asked_row, 0.0), axis=1, keepdims=True)
    table_row = iota((1, rows_dev), 1).astype(F32)
    hot_rows[...] = (table_row == asked_col).astype(F32).astype(BF16)

    found = nn(hot_rows[...], table_b[...]).astype(BF16)
    a_s[...] = found.reshape(shards, cap, E)
    d_r[shard] = a_s[shard]
    got = to_plane(0, a_s, d_r)
    hot = hot_rows[...]
    pairs = nt(hot, hot)
    earlier = jnp.sum(jnp.where(lane_i < row_i, pairs, 0.0), axis=1, keepdims=True)
    first = jnp.where(earlier < 0.5, 1.0, 0.0)
    pairs = pairs.astype(BF16)
    state = state_v[...]
    flat = jnp.concatenate([state[k : k + 1, :] for k in range(rows_dev // T)], axis=1)
    high = flat.astype(BF16)
    rest = flat - high.astype(F32)
    mid = rest.astype(BF16)
    low = (rest - mid.astype(F32)).astype(BF16)
    three = jnp.concatenate(
        [jnp.broadcast_to(t, (16, rows_dev)) for t in (high, mid, low)], axis=0
    )
    at_rows = nt(three, hot)
    at_row = at_rows[0:1] + at_rows[16:17] + at_rows[32:33]
    at_col = jnp.sum(jnp.where(diagonal, at_row, 0.0), axis=1, keepdims=True)
    drain_later = list(pending)
    arrive(got)
    for d in xd:
        pl.semaphore_signal(known, inc=1, device_id=xpeer(d), device_id_type=MESH)
    embedded = nn(of_token, d_r[...].reshape(T, E))
    cot = cot_v[...]
    chunks = far_first(n) + [0]
    hop_b = {}

    def early(normed, dpre_u, gated):
        wacc_b[0] = tn(normed, dpre_u).reshape(wacc_b.shape[1:])
        wacc_b[1] = tn(gated, cot).reshape(wacc_b.shape[1:])
        w1s_b[...] = wacc_b[other].astype(BF16)
        for d in chunks:
            hop_b[d] = start(
                [remote(w1s_b.at[uat(d)], w1r_b.at[uat(d)], p1s.at[1, d], p1r.at[1, d], cpeer)]
            )

    dx, normed, dpre, dng, dog = layer(
        embedded, cot, w, wout, ng[...], og[...], same, early
    )

    wide = wacc_a.shape[4]
    wacc_a[0] = tn(normed, dpre[:, :wide]).reshape(wacc_a.shape[1:])
    wacc_a[1] = tn(normed, dpre[:, wide:]).reshape(wacc_a.shape[1:])
    w1s_a[...] = wacc_a[other].astype(BF16)
    hop_a = {d: start([remote(w1s_a.at[vat(d)], w1r_a.at[vat(d)], p1s.at[0, d], p1r.at[0, d], cpeer)]) for d in chunks}
    pl.semaphore_wait(known, nx - 1)

    def over_x(k, hop, d, at, wacc, w1r, acc, w2s, w2r):
        arrive(hop[d])
        summed = wacc[c, at] + w1r[at].astype(F32)
        acc[at] = summed
        w2s[at] = summed.astype(BF16)
        hop[d] = start([
            remote(w2s.at[at, xat(e)], w2r.at[at, e - 1], p2s.at[k, d, e], p2r.at[k, d, e], xpeer(e))
            for e in xd
        ])

    for d in chunks:
        over_x(1, hop_b, d, vat(d), wacc_b, w1r_b, acc_b, w2s_b, w2r_b)
    ga_c[c] = jnp.concatenate([dng, dog, jnp.zeros((6, E), F32)], axis=0)
    got_ga = across(2, ga_c.at[c], ga_c.at[c])

    dx_high, dx_low = split2(dx)
    slot_grad = (nn(of_slot, dx_high) + nn(of_slot, dx_low)).astype(BF16)
    e_s[...] = slot_grad.reshape(shards, cap, E)
    g_r[shard] = e_s[shard]
    got_grad = to_plane(1, e_s, g_r)

    for d in chunks:
        over_x(0, hop_a, d, uat(d), wacc_a, w1r_a, acc_a, w2s_a, w2r_a)
    arrive(got_ga)
    ga_x[x] = ga_c[0] + ga_c[1]
    got_ga = along_x(0, lambda d: ga_x.at[x], lambda d: ga_x.at[x])
    for copy in drain_later:
        copy.wait_send()
    del pending[: len(drain_later)]
    got = [[], []]
    own = [None, None]
    for k, hop, at_of, acc, w2r, w3s, w3r, peer in (
        (1, hop_b, vat, acc_b, w2r_b, w3s_b, w3r_b, vshard),
        (0, hop_a, uat, acc_a, w2r_a, w3s_a, w3r_a, ushard),
    ):
        for d in chunks:
            at = at_of(d)
            arrive(hop[d])
            total = acc[at, x]
            for e in range(nx - 1):
                total = total + w2r[at, e].astype(F32)
            if d:
                w3s[d - 1] = total.astype(BF16)
                got[k] += start([
                    remote(w3s.at[d - 1], w3r.at[d - 1], p3s.at[k, d], p3r.at[k, d], {"shard": peer(d)})
                ])
            else:
                own[k] = total
    arrive(got_ga)
    gsum = ga_x[0]
    for k in range(1, nx):
        gsum = gsum + ga_x[k]
    ga_z[z] = gsum
    got_ga = along_z(1, lambda d: ga_z.at[z], lambda d: ga_z.at[z])

    arrive(got_grad)
    sums = nn(pairs, g_r[...].reshape(T, E))
    square = lane_mean(sums * sums)
    scale = (-LEARN_RATE) * first * lax.rsqrt(at_col + square + EPSILON)
    dall[rep] = (sums * scale).astype(BF16)
    square_row = jnp.sum(jnp.where(diagonal, square * first, 0.0), axis=0, keepdims=True)
    mall[rep] = jnp.concatenate([asked_row, square_row, jnp.zeros((6, T), F32)], axis=0)
    got_d = along_x(1, lambda d: dall.at[rep], lambda d: dall.at[rep])
    got_m = along_x(2, lambda d: mall.at[rep], lambda d: mall.at[rep])
    forwards = across(3, dall.at[rep], dall.at[rep]) + across(4, mall.at[rep], mall.at[rep])

    hop = [None, None]
    for k, w3r, w4, at, other_at in ((1, w3r_b, w4_b, upos, ushard), (0, w3r_a, w4_a, vpos, vshard)):
        arrive(got[k])
        total = own[k]
        for d in range(1, n):
            total = total + w3r[d - 1].astype(F32)
        w4[at] = total.astype(BF16)
        hop[k] = start([
            remote(w4.at[at], w4.at[at], p4s.at[k, d], p4r.at[k, d], {"shard": other_at(d)}) for d in far_first(n)
        ])
    arrive(got_ga)
    gsum = ga_z[0]
    for k in range(1, nz):
        gsum = gsum + ga_z[k]
    ga_y[y] = gsum
    got_ga = along_y(2, lambda d: ga_y.at[y], lambda d: ga_y.at[y])

    scale = 1.0 / math.sqrt(T * shards * reps)
    got = [None, None]
    mine = [None, None]
    for k, w4, fin, at, peer, s1, s2 in (
        (1, w4_b, fin_b, vx_at(0, 0), vx, bs, br), (0, w4_a, fin_a, ux_at(0, 0), ux, as_, ar)
    ):
        arrive(hop[k])
        total = w4[0].astype(F32)
        for j in range(1, n):
            total = total + w4[j].astype(F32)
        fin[c, at] = (total * scale).astype(BF16)
        mine[k] = fin.at[c, at]
        got[k] = start([
            remote(mine[k], mine[k], s1.at[a * nx + b], s2.at[a * nx + b], peer(a, b)) for a, b in box
        ])
    from_c = start([
        remote(mine[0], mine[0], gas.at[0], gar.at[0], cpeer),
        remote(mine[1], mine[1], gbs.at[0], gbr.at[0], cpeer),
    ])

    arrive(got_d)
    arrive(got_m)
    for d in range(1, nx):
        source = xat(nx - d) * 2 + c
        forwards += across(3 + 2 * d, dall.at[source], dall.at[source])
        forwards += across(4 + 2 * d, mall.at[source], mall.at[source])

    arrive(forwards)
    squares = jnp.concatenate([mall[k][1:2, :] for k in range(reps)], axis=1)
    sq_high, sq_low = split2(squares)
    both = jnp.concatenate([jnp.broadcast_to(t, (16, reps * T)) for t in (sq_high, sq_low)], axis=0)
    asked = jnp.concatenate([mall[k][0:1, :] for k in range(reps)], axis=1)
    changes = dall[...].reshape(reps * T, E)
    share = 1.0 / reps
    for block in range(rows_dev // T):
        row_id = (iota((T, 1), 0) + block * T).astype(F32)
        hot = (row_id == asked).astype(F32).astype(BF16)
        rows_out[block * T : (block + 1) * T, :] = nn(hot, changes) * share
        add = nt(both, hot)
        state_out[block : block + 1, :] = state[block : block + 1, :] + (add[0:1] + add[16:17]) * share

    arrive(got_ga)
    gsum = ga_y[0]
    for k in range(1, ny):
        gsum = gsum + ga_y[k]
    gains_out[...] = gsum * scale
    late = [id(copy) for copy in got[0] + got[1] + from_c]
    for copy in pending:
        if id(copy) not in late:
            copy.wait_send()
    pending[:] = [p for p in pending if id(p) in late]
    parts = [
        (hops(a, n) + hops(b, nx), k, a, b, copy) for k in range(2) for (a, b), copy in zip(box, got[k])
    ]
    parts.sort(key=lambda p: p[:4])
    for _, which, a, b, copy in parts:
        arrive([copy])
        copy.wait_send()
        pending[:] = [p for p in pending if p is not copy]
        e = a * nx + b
        if which == 0:
            part = fin_a.at[c, ux_at(n - a, nx - b)]
            from_c += start([remote(part, part, gas.at[e], gar.at[e], cpeer)])
        else:
            part = fin_b.at[c, vx_at(n - a, nx - b)]
            from_c += start([remote(part, part, gbs.at[e], gbr.at[e], cpeer)])
    arrive(from_c)
    drain()


def write_kernel(rows, state, fin_a, fin_b, gains, rows_o, state_o, uvqk_o, wout_o, gains_o, uvqk, wout, sem):
    first = pltpu.make_async_copy(rows, rows_o, sem.at[0])
    first.start()
    at = fin_a.shape[2]
    half = at + fin_b.shape[2]
    uvqk[:, : half - at] = fin_b[0].astype(F32)
    uvqk[:, half - at : half] = fin_a[0].astype(F32)
    uvqk[:, half:] = fin_a[1].astype(F32)
    second = pltpu.make_async_copy(uvqk, uvqk_o, sem.at[1])
    second.start()
    wout[...] = fin_b[1].astype(F32)
    third = pltpu.make_async_copy(wout, wout_o, sem.at[2])
    third.start()
    state_o[...] = state[...]
    gains_o[...] = gains[0:2, :]
    first.wait()
    second.wait()
    third.wait()


def on_device(nz, ny, nx, request_rows, token_slot, seq_lengths, cotangent, table_slab,
              adagrad_state, w_uvqk, w_out, norm_gain, out_gain):
    rows_dev = table_slab.shape[0]
    shards, reps = nz * ny, 2 * nx
    cap = T // shards
    ca, cb = nz * nx, ny * nx
    chunk_a, chunk_b = (E // ca, 384), (E // cb, 256)
    vmem = pl.BlockSpec(memory_space=pltpu.VMEM)
    hbm = pl.BlockSpec(memory_space=pltpu.HBM)
    dma = pltpu.SemaphoreType.DMA
    V = pltpu.VMEM
    I32 = jnp.int32
    rows, state, fin_a, fin_b, gains = pl.pallas_call(
        functools.partial(step_kernel, nz, ny, nx),
        out_shape=(
            jax.ShapeDtypeStruct((rows_dev, E), F32),
            jax.ShapeDtypeStruct((rows_dev // T, T), F32),
            jax.ShapeDtypeStruct((2, ca, *chunk_a), BF16),
            jax.ShapeDtypeStruct((2, cb, *chunk_b), BF16),
            jax.ShapeDtypeStruct((8, E), F32),
        ),
        in_specs=[hbm] * 10,
        out_specs=(vmem,) * 5,
        scratch_shapes=[
            pltpu.SMEM((1, SEQS), I32), V((1, 1, T), I32), V((1, T), I32), V((T, E), BF16),
            V((rows_dev, E), F32), V((rows_dev // T, T), F32), V((E, 4 * E), BF16), V((E, E), BF16),
            V((1, E), F32), V((1, E), F32),
            V((nz, 1, T), I32), V((ny, 1, T), I32),
            V((shards, cap, E), BF16), V((shards, cap, E), BF16),
            V((shards, cap, E), BF16), V((shards, cap, E), BF16),
            V((T, rows_dev), BF16), V((rows_dev, E), BF16),
            V((reps, T, E), BF16), V((reps, 8, T), F32),
            V((2, nz, nx, *chunk_a), F32), V((2, nz, nx, *chunk_b), F32),
            V((nz, nx, *chunk_a), BF16), V((nz, nx, *chunk_b), BF16),
            V((nz, nx, *chunk_a), BF16), V((nz, nx, *chunk_b), BF16),
            V((nz, nx, *chunk_a), F32), V((nz, nx, *chunk_b), F32),
            V((nz, nx, *chunk_a), BF16), V((nz, nx, *chunk_b), BF16),
            V((nz, nx - 1, *chunk_a), BF16), V((nz, nx - 1, *chunk_b), BF16),
            V((nz - 1, *chunk_a), BF16), V((nz - 1, *chunk_b), BF16),
            V((nz - 1, *chunk_a), BF16), V((nz - 1, *chunk_b), BF16),
            V((nz, *chunk_a), BF16), V((nz, *chunk_b), BF16),
            V((2, 8, E), F32), V((nx, 8, E), F32), V((nz, 8, E), F32), V((ny, 8, E), F32),
            dma((10,)),
            dma((3, nz)), dma((3, nz)), dma((3, ny)), dma((3, ny)),
            dma((3, nx)), dma((3, nx)), dma((3 + 2 * nx,)), dma((3 + 2 * nx,)),
            dma((2, shards)), dma((2, shards)),
            dma((2, nz)), dma((2, nz)), dma((2, nz, nx)), dma((2, nz, nx)),
            dma((2, nz)), dma((2, nz)), dma((2, nz)), dma((2, nz)),
            dma((ca,)), dma((ca,)), dma((cb,)), dma((cb,)),
            dma((ca,)), dma((ca,)), dma((cb,)), dma((cb,)),
            pltpu.SemaphoreType.REGULAR,
        ],
        compiler_params=pltpu.CompilerParams(
            collective_id=0, has_side_effects=True, vmem_limit_bytes=24 << 20
        ),
        name="step",
    )(
        *(
            pltpu.with_memory_space_constraint(a, pltpu.HBM)
            for a in (
                seq_lengths.reshape(1, SEQS),
                request_rows.reshape(1, 1, T),
                token_slot,
                cotangent[0],
                table_slab,
                adagrad_state.reshape(rows_dev // T, T),
                w_uvqk,
                w_out,
                norm_gain.reshape(1, E),
                out_gain.reshape(1, E),
            )
        )
    )
    rows, state, uvqk, wout, gains = pl.pallas_call(
        write_kernel,
        out_shape=(
            jax.ShapeDtypeStruct((rows_dev, E), F32),
            jax.ShapeDtypeStruct((rows_dev // T, T), F32),
            jax.ShapeDtypeStruct((E, 4 * E), F32),
            jax.ShapeDtypeStruct((E, E), F32),
            jax.ShapeDtypeStruct((2, E), F32),
        ),
        in_specs=[vmem] * 5,
        out_specs=(hbm, vmem, hbm, hbm, vmem),
        scratch_shapes=[V((E, 4 * E), F32), V((E, E), F32), dma((3,))],
        compiler_params=pltpu.CompilerParams(vmem_limit_bytes=24 << 20),
        name="write",
    )(rows, state, fin_a.reshape(2, E, 384), fin_b.reshape(2, E, 256), gains)
    return rows, state.reshape(rows_dev), uvqk, wout, gains


def solution(mesh):
    shards, reps = mesh.shape["shard"], mesh.shape["replica"]
    side = math.isqrt(shards)
    return jax.shard_map(
        functools.partial(on_device, side, shards // side, reps // 2),
        mesh=mesh,
        in_specs=(
            P("replica", "shard", None),
            P("replica", "shard"),
            P("replica", "shard", None),
            P("replica", "shard", None),
            P("shard", None),
            P("shard"),
            P(),
            P(),
            P(),
            P(),
        ),
        out_specs=(P("shard", None), P("shard"), P(), P(), P()),
        check_vma=False,
    )
```

```python
import functools
import math

import jax
import jax.numpy as jnp
from jax import lax
from jax.experimental import pallas as pl
from jax.experimental.pallas import tpu as pltpu
from jax.sharding import PartitionSpec as P

HEADS = 4
MAXLEN = 48
SEQS = 8
EPSILON = 1e-08
LEARN_RATE = 0.5
E = 256
T = 128
F32 = jnp.float32
BF16 = jnp.bfloat16
MESH = pl.DeviceIdType.MESH


def far_first(n):
    return sorted(range(1, n), key=lambda d: -min(d, n - d))


def nn(a, b):
    return lax.dot_general(a, b, (((1,), (0,)), ((), ())), preferred_element_type=F32)


def nt(a, b):
    return lax.dot_general(a, b, (((1,), (1,)), ((), ())), preferred_element_type=F32)


def tn(a, b):
    return lax.dot_general(a, b, (((0,), (0,)), ((), ())), preferred_element_type=F32)


def iota(shape, dim):
    return lax.broadcasted_iota(jnp.int32, shape, dim)


def lane_mean(x):
    return jnp.sum(x, axis=1, keepdims=True) * (1.0 / x.shape[1])


def split2(x):
    high = x.astype(BF16)
    return high, (x - high.astype(F32)).astype(BF16)


def layer(x, cot, w_ref, wout_ref, ng, og, same):
    center = x - lane_mean(x)
    rstd = lax.rsqrt(lane_mean(center * center) + 1e-05)
    xhat = center * rstd
    normed = (xhat * ng).astype(BF16)
    pre = nn(normed, w_ref[...])
    sig = lax.logistic(pre)
    proj = pre * sig
    dsilu = sig * (1.0 + pre * (1.0 - sig))
    u = proj[:, :E]
    low = iota((T, 128), 1) < 64
    zero = jnp.zeros((T, 128), BF16)
    pairs, att = [], []
    for p in range(2):
        at = p * 128
        vp = proj[:, E + at : E + at + 128].astype(BF16)
        qp = proj[:, 2 * E + at : 2 * E + at + 128].astype(BF16)
        kp = proj[:, 3 * E + at : 3 * E + at + 128].astype(BF16)
        heads, total = [], None
        for h in range(2):
            mine = low if h == 0 else jnp.logical_not(low)
            qh, kh = jnp.where(mine, qp, zero), jnp.where(mine, kp, zero)
            s = nt(qh, kp) * 0.125
            sg = lax.logistic(s)
            weights = jnp.where(same, s * sg * (1.0 / MAXLEN), 0.0).astype(BF16)
            slope = jnp.where(same, sg * (1.0 + s * (1.0 - sg)) * (0.125 / MAXLEN), 0.0)
            part = nn(weights, jnp.where(mine, vp, zero))
            total = part if total is None else total + part
            heads.append((mine, qh, kh, weights, slope))
        pairs.append((vp, heads))
        att.append(total)
    attended = jnp.concatenate(att, axis=1)
    center2 = attended - lane_mean(attended)
    rstd2 = lax.rsqrt(lane_mean(center2 * center2) + 1e-05)
    ahat = center2 * rstd2
    gated = (ahat * og * u).astype(BF16)
    dgated = nt(cot, wout_ref[...]).astype(BF16).astype(F32)
    au = ahat * u
    dog = jnp.sum(dgated * au, axis=0, keepdims=True)
    dgo = dgated * og
    du = dgo * ahat
    dahat = dgo * u
    datt = rstd2 * (dahat - lane_mean(dahat) - ahat * lane_mean(dahat * ahat))
    datt = datt.astype(BF16)
    dvs, dqs, dks = [], [], []
    for p in range(2):
        vp, heads = pairs[p]
        dp = datt[:, p * 128 : p * 128 + 128]
        dv = dq = dk = None
        for mine, qh, kh, weights, slope in heads:
            dh = jnp.where(mine, dp, zero)
            dw = nt(dh, vp).astype(BF16).astype(F32)
            ds = (dw * slope).astype(BF16)
            a, b, c = tn(weights, dh), nn(ds, kh), tn(ds, qh)
            dv, dq, dk = (a, b, c) if dv is None else (dv + a, dq + b, dk + c)
        dvs.append(dv)
        dqs.append(dq)
        dks.append(dk)
    rounded = [t.astype(BF16).astype(F32) for t in (*dvs, *dqs, *dks)]
    dproj = jnp.concatenate([du, *rounded], axis=1)
    dpre = (dproj * dsilu).astype(BF16)
    dnormed = nt(dpre, w_ref[...]).astype(BF16).astype(F32)
    dng = jnp.sum(dnormed * xhat, axis=0, keepdims=True)
    dxhat = dnormed * ng
    dx = rstd * (dxhat - lane_mean(dxhat) - xhat * lane_mean(dxhat * xhat)) + cot.astype(F32)
    return dx, normed, dpre, gated, dng, dog


def step_kernel(
    nz, ny, nx,
    lens_in, ids_in, slots_in, cot_in, table_in, state_in, w_in, wout_in, ng_in, og_in,
    rows_out, state_out, fin_out, gains_out,
    lens, ids, slots, cot_v, table, state_v, w, wout, ng, og,
    iz, iy, a_s, d_r, e_s, g_r, hot_rows, table_b,
    dall, mall, wacc, w1_s, w1_r, acc2, w2_s, w2_r, w3_s, w3_r, w4, fin,
    ga_c, ga_x, ga_z, ga_y,
    ls, zs, zr, ys, yr, xs, xr, cs, cr, rs_s, rs_r, p1s, p1r, p2s, p2r, gxs, gxr, gcs, gcr,
):
    shards, reps = nz * ny, 2 * nx
    cap = T // shards
    zb = T // nz
    lcap, lzb = int(math.log2(cap)), int(math.log2(zb))
    rows_dev = table.shape[0]
    shard, rep = lax.axis_index("shard"), lax.axis_index("replica")
    z, y = shard // ny, lax.rem(shard, ny)
    x, c = rep // 2, lax.rem(rep, 2)
    other = 1 - c
    zat = lambda d: lax.rem(z + d, nz)
    yat = lambda d: lax.rem(y + d, ny)
    xat = lambda d: lax.rem(x + d, nx)
    zpeer = lambda d: {"shard": zat(d) * ny + y}
    ypeer = lambda d: {"shard": z * ny + yat(d)}
    xpeer = lambda d: {"replica": xat(d) * 2 + c}
    cpeer = {"replica": x * 2 + other}
    zd, yd, xd = far_first(nz), far_first(ny), far_first(nx)
    hops = lambda d, n: min(d, n - d)
    plane = [(a, b) for a in range(nz) for b in range(ny) if a or b]
    plane.sort(key=lambda d: -(hops(d[0], nz) + hops(d[1], ny)))

    def remote(src, dst, ssem, rsem, peer):
        return pltpu.make_async_remote_copy(
            src_ref=src, dst_ref=dst, send_sem=ssem, recv_sem=rsem,
            device_id=peer, device_id_type=MESH,
        )

    pending = []

    def start(copies):
        for copy in copies:
            copy.start()
        pending.extend(copies)
        return copies

    def arrive(copies):
        for copy in copies:
            copy.wait_recv()

    def along_z(k, src, dst):
        return start([remote(src(d), dst(d), zs.at[k, d], zr.at[k, d], zpeer(d)) for d in zd])

    def along_y(k, src, dst):
        return start([remote(src(d), dst(d), ys.at[k, d], yr.at[k, d], ypeer(d)) for d in yd])

    def along_x(k, src, dst):
        return start([remote(src(d), dst(d), xs.at[k, d], xr.at[k, d], xpeer(d)) for d in xd])

    def across(k, src, dst):
        return start([remote(src, dst, cs.at[k], cr.at[k], cpeer)])

    def to_plane(k, src, dst):
        copies = []
        for a, b in plane:
            target = zat(a) * ny + yat(b)
            e = a * ny + b
            copies.append(
                remote(src.at[target], dst.at[shard], rs_s.at[k, e], rs_r.at[k, e], {"shard": target})
            )
        return start(copies)

    barrier = pltpu.get_barrier_semaphore()
    peers = [zpeer(d) for d in zd] + [ypeer(d) for d in yd] + [xpeer(d) for d in xd] + [cpeer]
    for peer in peers:
        pl.semaphore_signal(barrier, inc=1, device_id=peer, device_id_type=MESH)
    sources = (ids_in, lens_in, slots_in, state_in, ng_in, og_in, table_in, cot_in, w_in, wout_in)
    targets = (ids, lens, slots, state_v, ng, og, table, cot_v, w, wout)
    loads = [
        pltpu.make_async_copy(src, dst, ls.at[k]) for k, (src, dst) in enumerate(zip(sources, targets))
    ]
    for load in loads:
        load.start()

    for load in loads[:6]:
        load.wait()
    iz[z] = ids[0]
    row_i, lane_i = iota((T, T), 0), iota((T, T), 1)
    diagonal = row_i == lane_i
    ends = jnp.int32(0)
    seg_row = jnp.zeros((8, T), jnp.int32)
    seg_col = jnp.zeros((T, T), jnp.int32)
    row_t = iota((8, T), 1)
    for k in range(SEQS):
        ends = ends + lens[0, k]
        seg_row = seg_row + (row_t >= ends).astype(jnp.int32)
        seg_col = seg_col + (row_i >= ends).astype(jnp.int32)
    same = (seg_col == seg_row[0:1, :]) & (row_i >= lane_i)
    slot = slots[...].astype(F32)
    slot_col = jnp.sum(jnp.where(diagonal, slot, 0.0), axis=1, keepdims=True)
    of_slot = (row_i.astype(F32) == slot).astype(F32).astype(BF16)
    of_token = (lane_i.astype(F32) == slot_col).astype(F32).astype(BF16)

    pl.semaphore_wait(barrier, len(peers))

    got = along_z(0, lambda d: ids.at[0], lambda d: iz.at[z])
    loads[6].wait()
    table_b[...] = table[...].astype(BF16)
    arrive(got)
    total = jnp.zeros((8, T), jnp.int32)
    for s in range(nz):
        row = jnp.broadcast_to(iz[s], (8, T))
        row = jnp.where((row_t >> lzb) == z, row, 0)
        total = total + pltpu.roll(row, lax.rem((s - z) * zb + T, T), 1)
    iy[y] = total[0:1, :]
    got = along_y(0, lambda d: iy.at[y], lambda d: iy.at[y])
    for load in loads[7:]:
        load.wait()
    arrive(got)
    total = jnp.zeros((8, T), jnp.int32)
    for s in range(ny):
        row = jnp.broadcast_to(iy[s], (8, T))
        row = jnp.where(((row_t >> lcap) & (ny - 1)) == y, row, 0)
        total = total + pltpu.roll(row, lax.rem((s - y) * cap + T, T), 1)
    asked_row = total[0:1, :].astype(F32)
    asked_col = jnp.sum(jnp.where(diagonal, asked_row, 0.0), axis=1, keepdims=True)
    table_row = iota((1, rows_dev), 1).astype(F32)
    hot_rows[...] = (table_row == asked_col).astype(F32).astype(BF16)

    found = nn(hot_rows[...], table_b[...]).astype(BF16)
    a_s[...] = found.reshape(shards, cap, E)
    d_r[shard] = a_s[shard]
    got = to_plane(0, a_s, d_r)
    hot = hot_rows[...]
    pairs = nt(hot, hot)
    earlier = jnp.sum(jnp.where(lane_i < row_i, pairs, 0.0), axis=1, keepdims=True)
    first = jnp.where(earlier < 0.5, 1.0, 0.0)
    pairs = pairs.astype(BF16)
    state = state_v[...]
    flat = jnp.concatenate([state[k : k + 1, :] for k in range(rows_dev // T)], axis=1)
    high = flat.astype(BF16)
    rest = flat - high.astype(F32)
    mid = rest.astype(BF16)
    low = (rest - mid.astype(F32)).astype(BF16)
    three = jnp.concatenate(
        [jnp.broadcast_to(t, (16, rows_dev)) for t in (high, mid, low)], axis=0
    )
    at_rows = nt(three, hot)
    at_row = at_rows[0:1] + at_rows[16:17] + at_rows[32:33]
    at_col = jnp.sum(jnp.where(diagonal, at_row, 0.0), axis=1, keepdims=True)
    arrive(got)
    embedded = nn(of_token, d_r[...].reshape(T, E))
    cot = cot_v[...]
    dx, normed, dpre, gated, dng, dog = layer(
        embedded, cot, w, wout, ng[...], og[...], same
    )

    half = wacc.shape[4]
    shape = wacc.shape[1:]
    wacc[0] = tn(normed, dpre[:, :half]).reshape(shape)
    dwout = tn(gated, cot)
    wacc[1] = jnp.concatenate([tn(normed, dpre[:, half:]), dwout], axis=1).reshape(shape)
    w1_s[...] = wacc[other].astype(BF16)
    chunks = zd + [0]
    hop = {}
    for d in chunks:
        hop[d] = start([remote(w1_s.at[zat(d)], w1_r.at[zat(d)], p1s.at[d], p1r.at[d], cpeer)])
    ga_c[c] = jnp.concatenate([dng, dog, jnp.zeros((6, E), F32)], axis=0)
    got_ga = across(0, ga_c.at[c], ga_c.at[c])
    dx_high, dx_low = split2(dx)
    slot_grad = (nn(of_slot, dx_high) + nn(of_slot, dx_low)).astype(BF16)
    e_s[...] = slot_grad.reshape(shards, cap, E)
    g_r[shard] = e_s[shard]
    got_grad = to_plane(1, e_s, g_r)

    for d in chunks:
        arrive(hop[d])
        summed = wacc[c, zat(d)] + w1_r[zat(d)].astype(F32)
        acc2[zat(d)] = summed
        w2_s[zat(d)] = summed.astype(BF16)
        hop[d] = start([
            remote(w2_s.at[zat(d), xat(e)], w2_r.at[zat(d), e - 1], p2s.at[d, e], p2r.at[d, e], xpeer(e))
            for e in xd
        ])
    arrive(got_ga)
    ga_x[x] = ga_c[0] + ga_c[1]
    got_ga = along_x(0, lambda d: ga_x.at[x], lambda d: ga_x.at[x])
    got_w = []
    for d in chunks:
        arrive(hop[d])
        acc3 = acc2[zat(d), x]
        for e in range(nx - 1):
            acc3 = acc3 + w2_r[zat(d), e].astype(F32)
        if d:
            w3_s[d - 1] = acc3.astype(BF16)
            got_w += start([remote(w3_s.at[d - 1], w3_r.at[d - 1], zs.at[1, d], zr.at[1, d], zpeer(d))])
    arrive(got_ga)
    gsum = ga_x[0]
    for k in range(1, nx):
        gsum = gsum + ga_x[k]
    ga_z[z] = gsum
    got_ga = along_z(2, lambda d: ga_z.at[z], lambda d: ga_z.at[z])

    arrive(got_grad)
    sums = nn(pairs, g_r[...].reshape(T, E))
    square = lane_mean(sums * sums)
    scale = (-LEARN_RATE) * first * lax.rsqrt(at_col + square + EPSILON)
    dall[rep] = (sums * scale).astype(BF16)
    square_row = jnp.sum(jnp.where(diagonal, square * first, 0.0), axis=0, keepdims=True)
    mall[rep] = jnp.concatenate([asked_row, square_row, jnp.zeros((6, T), F32)], axis=0)
    got_d = along_x(1, lambda d: dall.at[rep], lambda d: dall.at[rep])
    got_m = along_x(2, lambda d: mall.at[rep], lambda d: mall.at[rep])
    forwards = across(1, dall.at[rep], dall.at[rep]) + across(2, mall.at[rep], mall.at[rep])

    arrive(got_w)
    for d in range(1, nz):
        acc3 = acc3 + w3_r[d - 1].astype(F32)
    w4[y] = acc3.astype(BF16)
    got_w = along_y(1, lambda d: w4.at[y], lambda d: w4.at[y])
    arrive(got_ga)
    gsum = ga_z[0]
    for k in range(1, nz):
        gsum = gsum + ga_z[k]
    ga_y[y] = gsum
    got_ga = along_y(2, lambda d: ga_y.at[y], lambda d: ga_y.at[y])

    arrive(got_d)
    arrive(got_m)
    for d in range(1, nx):
        source = xat(nx - d) * 2 + c
        forwards += across(1 + 2 * d, dall.at[source], dall.at[source])
        forwards += across(2 + 2 * d, mall.at[source], mall.at[source])

    arrive(got_w)
    scale = 1.0 / math.sqrt(T * shards * reps)
    acc5 = w4[0].astype(F32)
    for k in range(1, ny):
        acc5 = acc5 + w4[k].astype(F32)
    fin[c, z, x] = (acc5 * scale).astype(BF16)
    from_z = dict(zip(zd, along_z(3, lambda d: fin.at[c, z, x], lambda d: fin.at[c, z, x])))
    near = [0] + zd[::-1]

    def pass_on(d):
        at = zat(nz - d) if d else z
        chunk = fin.at[c, at, x]
        to_x = start([remote(chunk, chunk, gxs.at[d, e], gxr.at[d, e], xpeer(e)) for e in xd])
        to_c = start([remote(chunk, chunk, gcs.at[d, 0], gcr.at[d, 0], cpeer)])
        return to_x, to_c

    from_x, from_c = {}, []
    from_x[0], sent = pass_on(0)
    from_c += sent

    arrive(forwards)
    squares = jnp.concatenate([mall[k][1:2, :] for k in range(reps)], axis=1)
    sq_high, sq_low = split2(squares)
    both = jnp.concatenate([jnp.broadcast_to(t, (16, reps * T)) for t in (sq_high, sq_low)], axis=0)
    asked = jnp.concatenate([mall[k][0:1, :] for k in range(reps)], axis=1)
    changes = dall[...].reshape(reps * T, E)
    share = 1.0 / reps
    for block in range(rows_dev // T):
        row_id = (iota((T, 1), 0) + block * T).astype(F32)
        hot = (row_id == asked).astype(F32).astype(BF16)
        rows_out[block * T : (block + 1) * T, :] = nn(hot, changes) * share
        add = nt(both, hot)
        state_out[block : block + 1, :] = state[block : block + 1, :] + (add[0:1] + add[16:17]) * share

    for d in near[1:]:
        arrive([from_z[d]])
        from_x[d], sent = pass_on(d)
        from_c += sent
    arrive(got_ga)
    gsum = ga_y[0]
    for k in range(1, ny):
        gsum = gsum + ga_y[k]
    gains_out[...] = gsum * scale
    for d in near:
        at = zat(nz - d) if d else z
        for e, copy in zip(xd, from_x[d]):
            arrive([copy])
            chunk = fin.at[c, at, xat(nx - e)]
            from_c += start([remote(chunk, chunk, gcs.at[d, e], gcr.at[d, e], cpeer)])
    arrive(from_c)
    fin_out[...] = fin[...]
    for copy in pending:
        copy.wait_send()


def write_kernel(rows, state, fin, gains, rows_o, state_o, uvqk_o, wout_o, gains_o, uvqk, wout, sem):
    first = pltpu.make_async_copy(rows, rows_o, sem.at[0])
    first.start()
    width = fin.shape[2]
    uvqk[:, :width] = fin[0].astype(F32)
    uvqk[:, width:] = fin[1, :, : uvqk.shape[1] - width].astype(F32)
    second = pltpu.make_async_copy(uvqk, uvqk_o, sem.at[1])
    second.start()
    wout[...] = fin[1, :, uvqk.shape[1] - width :].astype(F32)
    third = pltpu.make_async_copy(wout, wout_o, sem.at[2])
    third.start()
    state_o[...] = state[...]
    gains_o[...] = gains[0:2, :]
    first.wait()
    second.wait()
    third.wait()


def on_device(nz, ny, nx, request_rows, token_slot, seq_lengths, cotangent, table_slab,
              adagrad_state, w_uvqk, w_out, norm_gain, out_gain):
    rows_dev = table_slab.shape[0]
    shards, reps = nz * ny, 2 * nx
    cap = T // shards
    chunk = (E // (nx * nz), 640)
    vmem = pl.BlockSpec(memory_space=pltpu.VMEM)
    hbm = pl.BlockSpec(memory_space=pltpu.HBM)
    dma = pltpu.SemaphoreType.DMA
    V = pltpu.VMEM
    I32 = jnp.int32
    rows, state, fin, gains = pl.pallas_call(
        functools.partial(step_kernel, nz, ny, nx),
        out_shape=(
            jax.ShapeDtypeStruct((rows_dev, E), F32),
            jax.ShapeDtypeStruct((rows_dev // T, T), F32),
            jax.ShapeDtypeStruct((2, nz, nx, *chunk), BF16),
            jax.ShapeDtypeStruct((8, E), F32),
        ),
        in_specs=[hbm] * 10,
        out_specs=(vmem,) * 4,
        scratch_shapes=[
            pltpu.SMEM((1, SEQS), I32), V((1, 1, T), I32), V((1, T), I32), V((T, E), BF16),
            V((rows_dev, E), F32), V((rows_dev // T, T), F32), V((E, 4 * E), BF16), V((E, E), BF16),
            V((1, E), F32), V((1, E), F32),
            V((nz, 1, T), I32), V((ny, 1, T), I32),
            V((shards, cap, E), BF16), V((shards, cap, E), BF16),
            V((shards, cap, E), BF16), V((shards, cap, E), BF16),
            V((T, rows_dev), BF16), V((rows_dev, E), BF16),
            V((reps, T, E), BF16), V((reps, 8, T), F32),
            V((2, nz, nx, *chunk), F32),
            V((nz, nx, *chunk), BF16), V((nz, nx, *chunk), BF16),
            V((nz, nx, *chunk), F32),
            V((nz, nx, *chunk), BF16), V((nz, nx - 1, *chunk), BF16),
            V((nz - 1, *chunk), BF16), V((nz - 1, *chunk), BF16),
            V((ny, *chunk), BF16),
            V((2, nz, nx, *chunk), BF16),
            V((2, 8, E), F32), V((nx, 8, E), F32), V((nz, 8, E), F32), V((ny, 8, E), F32),
            dma((10,)),
            dma((4, nz)), dma((4, nz)), dma((3, ny)), dma((3, ny)),
            dma((3, nx)), dma((3, nx)), dma((1 + 2 * nx,)), dma((1 + 2 * nx,)),
            dma((2, shards)), dma((2, shards)),
            dma((nz,)), dma((nz,)), dma((nz, nx)), dma((nz, nx)),
            dma((nz, nx)), dma((nz, nx)), dma((nz, nx)), dma((nz, nx)),
        ],
        compiler_params=pltpu.CompilerParams(
            collective_id=0, has_side_effects=True, vmem_limit_bytes=24 << 20
        ),
        name="step",
    )(
        *(
            pltpu.with_memory_space_constraint(a, pltpu.HBM)
            for a in (
                seq_lengths.reshape(1, SEQS),
                request_rows.reshape(1, 1, T),
                token_slot,
                cotangent[0],
                table_slab,
                adagrad_state.reshape(rows_dev // T, T),
                w_uvqk,
                w_out,
                norm_gain.reshape(1, E),
                out_gain.reshape(1, E),
            )
        )
    )
    rows, state, uvqk, wout, gains = pl.pallas_call(
        write_kernel,
        out_shape=(
            jax.ShapeDtypeStruct((rows_dev, E), F32),
            jax.ShapeDtypeStruct((rows_dev // T, T), F32),
            jax.ShapeDtypeStruct((E, 4 * E), F32),
            jax.ShapeDtypeStruct((E, E), F32),
            jax.ShapeDtypeStruct((2, E), F32),
        ),
        in_specs=[vmem] * 4,
        out_specs=(hbm, vmem, hbm, hbm, vmem),
        scratch_shapes=[V((E, 4 * E), F32), V((E, E), F32), dma((3,))],
        compiler_params=pltpu.CompilerParams(vmem_limit_bytes=24 << 20),
        name="write",
    )(rows, state, fin.reshape(2, E, 640), gains)
    return rows, state.reshape(rows_dev), uvqk, wout, gains


def solution(mesh):
    shards, reps = mesh.shape["shard"], mesh.shape["replica"]
    side = math.isqrt(shards)
    return jax.shard_map(
        functools.partial(on_device, side, shards // side, reps // 2),
        mesh=mesh,
        in_specs=(
            P("replica", "shard", None),
            P("replica", "shard"),
            P("replica", "shard", None),
            P("replica", "shard", None),
            P("shard", None),
            P("shard"),
            P(),
            P(),
            P(),
            P(),
        ),
        out_specs=(P("shard", None), P("shard"), P(), P(), P()),
        check_vma=False,
    )
```
